32 devices in a mesh: feat: 8 (over z, core), col: 4 (over y, x).
Axes of the slice: x: 2, y: 2, z: 4, core: 2. Of those that a mesh axis runs over, the one named last changes fastest.
Arguments:
- self_feats: bfloat16 [4096, 128], P(('feat', 'col')), may hold values from -6 to 6
- neighbour_feats: bfloat16 [128, 16384], P('feat', 'col'), may hold values from -6 to 6
- tiles: bfloat16 [1024, 128, 128], P('col'), may hold values from 0 to 1, as said below
- tile_rows: int32 [1024], P('col'), may hold values from 0 to 31, as said below
- tile_cols: int32 [1024], P('col'), may hold values from 0 to 31
- tile_count: int32 [4], P('col'), may hold values from 1 to 256, 768 in all
- owner_order: int32 [32], replicated, may hold values from 0 to 31, as said below
- degree: int32 [4096], P(('feat', 'col')), may hold values from 64 to 192
- w_self: bfloat16 [128, 256], replicated, may hold values from -0.5 to 0.5
- w_neigh: bfloat16 [128, 256], replicated, may hold values from -0.5 to 0.5
- bias: float32 [256], replicated, may hold values from -3 to 3
- upstream: bfloat16 [4096, 256], P(('feat', 'col')), may hold values from -6 to 6
Outputs:
- hidden_out: bfloat16 [4096, 256], P(('feat', 'col'))
- neigh_grad: bfloat16 [128, 16384], P('feat', 'col')
The draws below stay inside these ranges and needn't reach their ends.
Inputs may be any that keep to these rules, and one draw needn't show every extreme that they name: `tiles`: every entry is 0 or 1. `tile_count`: slots at or after a group's count are ignored; some group has all 256 slots live. `owner_order`: a permutation of the row blocks. `tile_rows`: in every column group, slot s has a row block whose owner position p satisfies (p) % 4 == s % 4.
All inputs are finite; a program needn't handle non-finite values.
Results may differ from the reference program's by a relative error of at most 0.0065.
Values may be sent and summed in bfloat16 or wider, within the bound.
No kernel may reach another device: no remote copies, remote signals or barrier semaphores. Data moves between devices by JAX's collectives and lax.ppermute only.
A program may use at most 64 MiB of HBM per device.

```python
import math
import jax
import jax.numpy as jnp
import numpy as np
from jax import lax

F = 128
H = 256
TILE = 128
NT = 256
CB = 32
RBD = 1
RB = 32
ROWS = 4096
NCN = 16384
N_COL = 4


def shared_order(key):
    return jax.random.permutation(jax.random.fold_in(key, 11), RB).astype(jnp.int32)


def draw_owner_order(key, part):
    return shared_order(key)


def draw_tile_rows(key, part):
    order = shared_order(key)
    slot_ids = jnp.arange(N_COL * NT, dtype=jnp.int32)
    column_owner = slot_ids % NT % N_COL
    feat_owner = jax.random.randint(jax.random.fold_in(key, 12), (N_COL * NT,), 0, RB // (N_COL * RBD))
    within = jax.random.randint(jax.random.fold_in(key, 13), (N_COL * NT,), 0, RBD)
    position = (feat_owner * N_COL + column_owner) * RBD + within
    return order[position]


def draw_tiles(key, part):
    values = jax.random.randint(key, (N_COL * NT, TILE, TILE), 0, 4)
    return (values == 0).astype(jnp.float32).astype(jnp.bfloat16)


def place_ends(drawn, own_key, least, largest):
    spot = [jax.random.randint(jax.random.fold_in(own_key, axis), (), 0, length) for axis, length in enumerate(drawn.shape)]
    longest = drawn.shape.index(max(drawn.shape))
    beside = spot[:longest] + [(spot[longest] + 1) % drawn.shape[longest]] + spot[longest + 1:]
    return drawn.at[tuple(spot)].set(least).at[tuple(beside)].set(largest)


def block_levels(stream_key, dims, shards, least, largest):
    loudness = 1.0
    for dim, parts in shards:
        draws = jax.random.uniform(jax.random.fold_in(jax.random.fold_in(stream_key, 6), dim), (parts,), jnp.float32, least / len(shards), largest / len(shards))
        loudness = loudness * jnp.repeat(jnp.exp(draws), dims[dim] // parts).reshape((-1,) + (1,) * (len(dims) - 1 - dim))
    return loudness


def profile(amount, total, limit, skew):
    portions = [(1 << 20) // math.isqrt(rank ** skew) + 1 for rank in range(2, amount + 1)]
    surplus, holding = total - limit - (amount - 1), [1] * (amount - 1)
    while surplus > 0:
        candidates = [i for i in range(amount - 1) if holding[i] < limit]
        mass, budget = sum([portions[i] for i in candidates]), surplus
        for i in candidates:
            extra = min(limit - holding[i], max(1, budget * portions[i] // mass), surplus)
            holding[i] = holding[i] + extra
            surplus = surplus - extra
    return np.array([limit] + holding)


def ragged_sizes(rng, count, total, reach, skew):
    if count == 2:
        one = jax.random.randint(rng, (), max(1, total - reach), min(reach, total - 1) + 1)
        return jnp.stack([one, total - one])
    tallies = jnp.asarray(profile(count, total, reach, skew), jnp.int32)
    twos = (count - 1) // 2
    donor, receiver = tallies[1:1 + 2 * twos:2], tallies[2:2 + 2 * twos:2]
    slack = jnp.minimum(donor - 1, reach - receiver)
    shifted = jax.random.randint(jax.random.fold_in(rng, 1), (twos,), 0, 1 << 20) % (slack + 1)
    tallies = tallies.at[1:1 + 2 * twos:2].set(donor - shifted).at[2:2 + 2 * twos:2].set(receiver + shifted)
    return tallies[jax.random.permutation(jax.random.fold_in(rng, 2), count)]


def centred(key, extent, scale, most, shards=(), kind=jnp.bfloat16):
    values = jax.random.normal(key, extent, jnp.float32) * scale
    if len(shards) > 0:
        values = block_levels(key, extent, shards, -0.22, 0.18) * values
    return jnp.clip(values, min=-most, max=most).astype(kind)


def setup_inputs(seed: int = 0) -> dict:
    keys = jax.random.split(jax.random.key(seed), 13)
    return {
        "self_feats": centred(keys[0], (ROWS, F), 1.0, 6.0, ((0, 32),)),
        "neighbour_feats": centred(keys[1], (F, NCN), 1.0, 6.0, ((0, 8), (1, 4))),
        "tiles": draw_tiles(jax.random.fold_in(keys[12], 71), 0),
        "tile_rows": draw_tile_rows(jax.random.fold_in(keys[12], 71), 0),
        "tile_cols": place_ends(jax.random.randint(keys[4], (N_COL * NT,), 0, CB), jax.random.fold_in(keys[4], 1), 0, CB - 1).astype(jnp.int32),
        "tile_count": ragged_sizes(keys[5], N_COL, 3 * N_COL * NT // 4, NT, 2).astype(jnp.int32),
        "owner_order": draw_owner_order(jax.random.fold_in(keys[12], 71), 0),
        "degree": place_ends(jax.random.randint(keys[7], (ROWS,), 64, 193), jax.random.fold_in(keys[7], 1), 64, 192).astype(jnp.int32),
        "w_self": centred(keys[8], (F, H), F ** -0.5, 0.5),
        "w_neigh": centred(keys[9], (F, H), F ** -0.5, 0.5),
        "bias": centred(keys[10], (H,), 0.5, 3.0, (), jnp.float32),
        "upstream": centred(keys[11], (ROWS, H), 1.0, 6.0, ((0, 32),)),
    }


def reference(self_feats, neighbour_feats, tiles, tile_rows, tile_cols, tile_count, owner_order, degree, w_self, w_neigh, bias, upstream):
    places = jnp.zeros((RB,), jnp.int32).at[owner_order].set(jnp.arange(RB, dtype=jnp.int32))
    slot_ids = jnp.arange(NT, dtype=jnp.int32)

    def group_data(group):
        start = (group * NT).astype(jnp.int32)
        group_tiles = lax.dynamic_slice_in_dim(tiles, start, NT, 0).astype(jnp.float32)
        group_rows = lax.dynamic_slice_in_dim(tile_rows, start, NT, 0)
        group_cols = lax.dynamic_slice_in_dim(tile_cols, start, NT, 0)
        live = (slot_ids < tile_count[group]).astype(jnp.float32)
        return (group_tiles, places[group_rows], group_cols, live)

    def forward_group(total, group):
        group_tiles, target, group_cols, live = group_data(group)
        cstart = (group * CB * TILE).astype(jnp.int32)
        feats = lax.dynamic_slice_in_dim(neighbour_feats, cstart, CB * TILE, 1)
        blocked = feats.reshape(F, CB, TILE).transpose(1, 0, 2).astype(jnp.float32)
        picked = blocked[group_cols]
        products = jnp.einsum('nfk,nrk->nfr', picked, group_tiles) * live[:, None, None]
        return (total.at[target].add(products), None)
    groups = jnp.arange(N_COL, dtype=jnp.int32)
    summed_blocks, _ = lax.scan(forward_group, jnp.zeros((RB, F, TILE), jnp.float32), groups)
    summed = summed_blocks.transpose(0, 2, 1).reshape(ROWS, F)
    scale = lax.rsqrt(degree.astype(jnp.float32))[:, None]
    aggregate = (summed * scale).astype(jnp.bfloat16)
    pre = jnp.dot(self_feats, w_self, preferred_element_type=jnp.float32)
    pre = pre + jnp.dot(aggregate, w_neigh, preferred_element_type=jnp.float32) + bias
    gate = jax.nn.sigmoid(pre)
    hidden_out = (pre * gate).astype(jnp.bfloat16)
    slope = gate * (1.0 + pre * (1.0 - gate))
    dpre = (upstream.astype(jnp.float32) * slope).astype(jnp.bfloat16)
    dagg = jnp.dot(dpre, w_neigh.T, preferred_element_type=jnp.float32)
    back = (dagg * scale).astype(jnp.bfloat16)
    back_blocks = back.reshape(RB, TILE, F).transpose(0, 2, 1).astype(jnp.float32)

    def backward_group(carry, group):
        group_tiles, target, group_cols, live = group_data(group)
        taken = back_blocks[target]
        pieces = jnp.einsum('nfr,nrk->nfk', taken, group_tiles) * live[:, None, None]
        grads = jnp.zeros((CB, F, TILE), jnp.float32).at[group_cols].add(pieces)
        return (carry, grads.transpose(1, 0, 2).reshape(F, CB * TILE))
    _, per_group = lax.scan(backward_group, jnp.zeros((), jnp.float32), groups)
    neigh_grad = per_group.transpose(1, 0, 2).reshape(F, NCN).astype(jnp.bfloat16)
    return (hidden_out, neigh_grad)
```

```python
import functools

import jax
import jax.numpy as jnp
from jax import lax
from jax.experimental import pallas as pl
from jax.experimental.pallas import tpu as pltpu
from jax.sharding import PartitionSpec as P

CHUNK = 32
LANES = 4


def invert_order(order_ref, places):
    def body(position, carry):
        places[order_ref[position]] = position
        return carry

    lax.fori_loop(0, order_ref.shape[0], body, 0, unroll=8)


def tile_copy(tiles_hbm, tiles_vmem, sems, chunk):
    window = pl.ds(chunk * CHUNK, CHUNK)
    return pltpu.make_async_copy(tiles_hbm.at[window], tiles_vmem.at[window], sems.at[chunk])


def forward_kernel(
    rows_ref,
    cols_ref,
    count_ref,
    order_ref,
    feats_ref,
    tiles_hbm,
    partial_ref,
    tiles_ref,
    places,
    acc,
    sems,
):
    slots, tile_size, _ = tiles_ref.shape
    chunks = slots // CHUNK
    for chunk in range(chunks):
        tile_copy(tiles_hbm, tiles_ref, sems, chunk).start()
    invert_order(order_ref, places)
    acc[...] = jnp.zeros_like(acc)
    blocks_total = partial_ref.shape[0]
    count = count_ref[0]

    for chunk in range(chunks):
        tile_copy(tiles_hbm, tiles_ref, sems, chunk).wait()

        @pl.when(chunk * CHUNK < count)
        def _():
            for step in range(CHUNK):
                slot = chunk * CHUNK + step
                col = pl.multiple_of(cols_ref[slot] * tile_size, tile_size)
                target = jnp.where(slot < count, places[rows_ref[slot]], blocks_total)
                acc[target] += lax.dot_general(
                    feats_ref[:, pl.ds(col, tile_size)],
                    tiles_ref[slot],
                    (((1,), (1,)), ((), ())),
                    preferred_element_type=jnp.float32,
                )

    partial_ref[...] = acc[:blocks_total].astype(partial_ref.dtype)


def dense_kernel(
    got_ref,
    self_ref,
    degree_ref,
    w_self_ref,
    w_neigh_ref,
    bias_ref,
    upstream_ref,
    hidden_ref,
    back_ref,
    summed,
):
    nfeat, ncol, slice_width, tile_size = got_ref.shape
    for f in range(nfeat):
        summed[pl.ds(f * slice_width, slice_width), :] = jnp.sum(
            got_ref[f].astype(jnp.float32), axis=0
        )
    scale = lax.rsqrt(degree_ref[...].astype(jnp.float32))
    aggregate = (summed[...] * scale).astype(jnp.bfloat16)
    pre = jnp.dot(self_ref[...], w_self_ref[...], preferred_element_type=jnp.float32)
    pre = pre + lax.dot_general(
        aggregate, w_neigh_ref[...], (((0,), (0,)), ((), ())), preferred_element_type=jnp.float32
    )
    pre = pre + bias_ref[...]
    gate = jax.nn.sigmoid(pre)
    hidden_ref[...] = (pre * gate).astype(jnp.bfloat16)
    slope = gate * (1.0 + pre * (1.0 - gate))
    dpre = (upstream_ref[...].astype(jnp.float32) * slope).astype(jnp.bfloat16)
    dagg = lax.dot_general(
        w_neigh_ref[...], dpre, (((1,), (1,)), ((), ())), preferred_element_type=jnp.float32
    )
    back = dagg * scale
    for f in range(nfeat):
        piece = back[f * slice_width : (f + 1) * slice_width].astype(jnp.bfloat16)
        for c in range(ncol):
            back_ref[f, c] = piece


def backward_kernel(
    rows_ref,
    cols_ref,
    count_ref,
    order_ref,
    grads_ref,
    tiles_ref,
    out_ref,
    places,
    acc,
):
    slots, tile_size, _ = tiles_ref.shape
    chunks = slots // CHUNK
    invert_order(order_ref, places)
    acc[...] = jnp.zeros_like(acc)
    col_blocks = out_ref.shape[1] // tile_size
    count = count_ref[0]

    for chunk in range(chunks):

        @pl.when(chunk * CHUNK < count)
        def _():
            for step in range(CHUNK):
                slot = chunk * CHUNK + step
                source = places[rows_ref[slot]]
                target = jnp.where(slot < count, cols_ref[slot], col_blocks)
                acc[step % LANES, target] += jnp.dot(
                    grads_ref[source], tiles_ref[slot], preferred_element_type=jnp.float32
                )

    for block in range(col_blocks):
        total = acc[0, block]
        for lane in range(1, LANES):
            total = total + acc[lane, block]
        out_ref[:, block * tile_size : (block + 1) * tile_size] = total.astype(out_ref.dtype)


VMEM = pl.BlockSpec(memory_space=pltpu.VMEM)
SMEM = pl.BlockSpec(memory_space=pltpu.SMEM)
ANY = pl.BlockSpec(memory_space=pl.ANY)


def local(
    self_feats,
    neighbour_feats,
    tiles,
    tile_rows,
    tile_cols,
    tile_count,
    owner_order,
    degree,
    w_self,
    w_neigh,
    bias,
    upstream,
):
    nfeat = lax.axis_size("feat")
    ncol = lax.axis_size("col")
    slots, tile_size, _ = tiles.shape
    slice_width, width = neighbour_feats.shape
    col_blocks = width // tile_size
    rows = self_feats.shape[0]
    blocks_total = owner_order.shape[0]
    assert rows == tile_size and blocks_total == nfeat * ncol
    params = pltpu.CompilerParams(vmem_limit_bytes=48 << 20)

    partial_value, tiles_kept = pl.pallas_call(
        forward_kernel,
        out_shape=(
            jax.ShapeDtypeStruct((blocks_total, slice_width, tile_size), jnp.bfloat16),
            pltpu.VMEM(tiles.shape, tiles.dtype),
        ),
        in_specs=[SMEM, SMEM, SMEM, SMEM, VMEM, ANY],
        out_specs=(VMEM, VMEM),
        scratch_shapes=[
            pltpu.SMEM((blocks_total,), jnp.int32),
            pltpu.VMEM((blocks_total + 1, slice_width, tile_size), jnp.float32),
            pltpu.SemaphoreType.DMA((slots // CHUNK,)),
        ],
        compiler_params=params,
        name="forward",
    )(tile_rows, tile_cols, tile_count, owner_order, neighbour_feats, tiles)

    got = lax.all_to_all(partial_value, ("feat", "col"), split_axis=0, concat_axis=0, tiled=True)

    hidden_out, back = pl.pallas_call(
        dense_kernel,
        out_shape=(
            jax.ShapeDtypeStruct(upstream.shape, jnp.bfloat16),
            jax.ShapeDtypeStruct((nfeat, ncol, slice_width, tile_size), jnp.bfloat16),
        ),
        in_specs=[VMEM] * 7,
        out_specs=(VMEM, VMEM),
        scratch_shapes=[pltpu.VMEM((nfeat * slice_width, tile_size), jnp.float32)],
        compiler_params=params,
        name="dense",
    )(
        got.reshape(nfeat, ncol, slice_width, tile_size),
        self_feats,
        degree.reshape(1, rows),
        w_self,
        w_neigh,
        bias.reshape(1, -1),
        upstream,
    )

    row_grads = lax.all_to_all(
        back.reshape(blocks_total, slice_width, tile_size),
        ("feat", "col"),
        split_axis=0,
        concat_axis=0,
        tiled=True,
    )

    neigh_grad = pl.pallas_call(
        backward_kernel,
        out_shape=jax.ShapeDtypeStruct(neighbour_feats.shape, jnp.bfloat16),
        in_specs=[SMEM, SMEM, SMEM, SMEM, VMEM, VMEM],
        out_specs=VMEM,
        scratch_shapes=[
            pltpu.SMEM((blocks_total,), jnp.int32),
            pltpu.VMEM((LANES, col_blocks + 1, slice_width, tile_size), jnp.float32),
        ],
        compiler_params=params,
        name="backward",
    )(
        tile_rows,
        tile_cols,
        tile_count,
        owner_order,
        row_grads,
        pltpu.with_memory_space_constraint(tiles_kept, pltpu.VMEM),
    )
    return (hidden_out, neigh_grad)


def solution(mesh):
    in_specs = (
        P(("feat", "col"), None),
        P("feat", "col"),
        P("col", None, None),
        P("col"),
        P("col"),
        P("col"),
        P(),
        P(("feat", "col")),
        P(),
        P(),
        P(),
        P(("feat", "col"), None),
    )
    out_specs = (P(("feat", "col"), None), P("feat", "col"))
    return jax.shard_map(local, mesh=mesh, in_specs=in_specs, out_specs=out_specs, check_vma=False)
```

```python
import jax
import jax.numpy as jnp
from jax import lax
from jax.experimental import pallas as pl
from jax.experimental.pallas import tpu as pltpu
from jax.sharding import PartitionSpec as P

CHUNK = 64
STACK = 8


def invert_order(order_ref, places):
    def body(position, carry):
        places[order_ref[position]] = position
        return carry

    lax.fori_loop(0, order_ref.shape[0], body, 0, unroll=8)


def tile_copy(tiles_hbm, tiles_vmem, sems, chunk):
    window = pl.ds(chunk * CHUNK, CHUNK)
    return pltpu.make_async_copy(tiles_hbm.at[window], tiles_vmem.at[window], sems.at[chunk])


def forward_kernel(
    rows_ref,
    cols_ref,
    count_ref,
    order_ref,
    feats_ref,
    tiles_hbm,
    partial_ref,
    tiles_ref,
    places,
    acc,
    sems,
):
    slots, tile_size, _ = tiles_ref.shape
    blocks_total, slice_width, _ = partial_ref.shape
    for chunk in range(slots // CHUNK):
        tile_copy(tiles_hbm, tiles_ref, sems, chunk).start()
    invert_order(order_ref, places)
    acc[...] = jnp.zeros_like(acc)
    count = count_ref[0]

    for first in range(0, slots, STACK):
        if first % CHUNK == 0:
            tile_copy(tiles_hbm, tiles_ref, sems, first // CHUNK).wait()
        group = range(first, first + STACK)
        starts = [pl.multiple_of(cols_ref[slot] * tile_size, tile_size) for slot in group]
        stacked = jnp.concatenate(
            [feats_ref[:, pl.ds(start, tile_size)] for start in starts], axis=0
        )
        crossed = lax.dot_general(
            stacked,
            tiles_ref[pl.ds(first, STACK)].reshape(STACK * tile_size, tile_size),
            (((1,), (1,)), ((), ())),
            preferred_element_type=jnp.float32,
        )
        for i, slot in enumerate(group):
            target = jnp.where(slot < count, places[rows_ref[slot]], blocks_total)
            acc[target] += crossed[
                i * slice_width : (i + 1) * slice_width, i * tile_size : (i + 1) * tile_size
            ]

    partial_ref[...] = acc[:blocks_total].astype(partial_ref.dtype)


def dense_kernel(
    got_ref,
    self_ref,
    degree_ref,
    w_self_ref,
    w_neigh_ref,
    bias_ref,
    upstream_ref,
    hidden_ref,
    back_ref,
    summed,
):
    nfeat, ncol, slice_width, tile_size = got_ref.shape
    for f in range(nfeat):
        summed[pl.ds(f * slice_width, slice_width), :] = jnp.sum(
            got_ref[f].astype(jnp.float32), axis=0
        )
    scale = lax.rsqrt(degree_ref[...].astype(jnp.float32))
    aggregate = (summed[...] * scale).astype(jnp.bfloat16)
    pre = jnp.dot(self_ref[...], w_self_ref[...], preferred_element_type=jnp.float32)
    pre = pre + lax.dot_general(
        aggregate, w_neigh_ref[...], (((0,), (0,)), ((), ())), preferred_element_type=jnp.float32
    )
    pre = pre + bias_ref[...]
    gate = jax.nn.sigmoid(pre)
    hidden_ref[...] = (pre * gate).astype(jnp.bfloat16)
    slope = gate * (1.0 + pre * (1.0 - gate))
    dpre = (upstream_ref[...].astype(jnp.float32) * slope).astype(jnp.bfloat16)
    dagg = lax.dot_general(
        w_neigh_ref[...], dpre, (((1,), (1,)), ((), ())), preferred_element_type=jnp.float32
    )
    back = dagg * scale
    for f in range(nfeat):
        piece = back[f * slice_width : (f + 1) * slice_width].astype(jnp.bfloat16)
        for c in range(ncol):
            back_ref[f, c] = piece


def backward_kernel(
    rows_ref,
    cols_ref,
    count_ref,
    order_ref,
    grads_ref,
    tiles_ref,
    out_ref,
    places,
    acc_even,
    acc_odd,
):
    slots, tile_size, _ = tiles_ref.shape
    slice_width = out_ref.shape[0]
    invert_order(order_ref, places)
    accs = (acc_even, acc_odd)
    for acc in accs:
        acc[...] = jnp.zeros_like(acc)
    col_blocks = out_ref.shape[1] // tile_size
    count = count_ref[0]
    blank = jnp.zeros((slice_width, tile_size), grads_ref.dtype)

    for first in range(0, slots, 2):
        even = grads_ref[places[rows_ref[first]]]
        odd = grads_ref[places[rows_ref[first + 1]]]
        diagonal = jnp.concatenate(
            [
                jnp.concatenate([even, blank], axis=1),
                jnp.concatenate([blank, odd], axis=1),
            ],
            axis=0,
        )
        pieces = jnp.dot(
            diagonal,
            tiles_ref[pl.ds(first, 2)].reshape(2 * tile_size, tile_size),
            preferred_element_type=jnp.float32,
        )
        for i, acc in enumerate(accs):
            target = jnp.where(first + i < count, cols_ref[first + i], col_blocks)
            acc[target] += pieces[i * slice_width : (i + 1) * slice_width]

    for block in range(col_blocks):
        total = acc_even[block] + acc_odd[block]
        out_ref[:, block * tile_size : (block + 1) * tile_size] = total.astype(out_ref.dtype)


VMEM = pl.BlockSpec(memory_space=pltpu.VMEM)
SMEM = pl.BlockSpec(memory_space=pltpu.SMEM)
ANY = pl.BlockSpec(memory_space=pl.ANY)


def local(
    self_feats,
    neighbour_feats,
    tiles,
    tile_rows,
    tile_cols,
    tile_count,
    owner_order,
    degree,
    w_self,
    w_neigh,
    bias,
    upstream,
):
    nfeat = lax.axis_size("feat")
    ncol = lax.axis_size("col")
    slots, tile_size, _ = tiles.shape
    slice_width, width = neighbour_feats.shape
    col_blocks = width // tile_size
    rows = self_feats.shape[0]
    blocks_total = owner_order.shape[0]
    assert rows == tile_size and blocks_total == nfeat * ncol
    params = pltpu.CompilerParams(vmem_limit_bytes=32 << 20)

    partial_value, tiles_kept = pl.pallas_call(
        forward_kernel,
        out_shape=(
            jax.ShapeDtypeStruct((blocks_total, slice_width, tile_size), jnp.bfloat16),
            pltpu.VMEM(tiles.shape, tiles.dtype),
        ),
        in_specs=[SMEM, SMEM, SMEM, SMEM, VMEM, ANY],
        out_specs=(VMEM, VMEM),
        scratch_shapes=[
            pltpu.SMEM((blocks_total,), jnp.int32),
            pltpu.VMEM((blocks_total + 1, slice_width, tile_size), jnp.float32),
            pltpu.SemaphoreType.DMA((slots // CHUNK,)),
        ],
        compiler_params=params,
        name="forward",
    )(tile_rows, tile_cols, tile_count, owner_order, neighbour_feats, tiles)

    got = lax.all_to_all(partial_value, ("feat", "col"), split_axis=0, concat_axis=0, tiled=True)

    hidden_out, back = pl.pallas_call(
        dense_kernel,
        out_shape=(
            jax.ShapeDtypeStruct(upstream.shape, jnp.bfloat16),
            jax.ShapeDtypeStruct((nfeat, ncol, slice_width, tile_size), jnp.bfloat16),
        ),
        in_specs=[VMEM] * 7,
        out_specs=(VMEM, VMEM),
        scratch_shapes=[pltpu.VMEM((nfeat * slice_width, tile_size), jnp.float32)],
        compiler_params=params,
        name="dense",
    )(
        got.reshape(nfeat, ncol, slice_width, tile_size),
        self_feats,
        degree.reshape(1, rows),
        w_self,
        w_neigh,
        bias.reshape(1, -1),
        upstream,
    )

    row_grads = lax.all_to_all(
        back.reshape(blocks_total, slice_width, tile_size),
        ("feat", "col"),
        split_axis=0,
        concat_axis=0,
        tiled=True,
    )

    neigh_grad = pl.pallas_call(
        backward_kernel,
        out_shape=jax.ShapeDtypeStruct(neighbour_feats.shape, jnp.bfloat16),
        in_specs=[SMEM, SMEM, SMEM, SMEM, VMEM, VMEM],
        out_specs=VMEM,
        scratch_shapes=[
            pltpu.SMEM((blocks_total,), jnp.int32),
            pltpu.VMEM((col_blocks + 1, slice_width, tile_size), jnp.float32),
            pltpu.VMEM((col_blocks + 1, slice_width, tile_size), jnp.float32),
        ],
        compiler_params=params,
        name="backward",
    )(
        tile_rows,
        tile_cols,
        tile_count,
        owner_order,
        row_grads,
        pltpu.with_memory_space_constraint(tiles_kept, pltpu.VMEM),
    )
    return (hidden_out, neigh_grad)


def solution(mesh):
    in_specs = (
        P(("feat", "col"), None),
        P("feat", "col"),
        P("col", None, None),
        P("col"),
        P("col"),
        P("col"),
        P(),
        P(("feat", "col")),
        P(),
        P(),
        P(),
        P(("feat", "col"), None),
    )
    out_specs = (P(("feat", "col"), None), P("feat", "col"))
    return jax.shard_map(local, mesh=mesh, in_specs=in_specs, out_specs=out_specs, check_vma=False)
```

```python
import jax
import jax.numpy as jnp
from jax import lax
from jax.experimental import pallas as pl
from jax.experimental.pallas import tpu as pltpu
from jax.sharding import PartitionSpec as P

CHUNK = 64
STACK = 8


def invert_order(order_ref, places):
    def body(position, carry):
        places[order_ref[position]] = position
        return carry

    lax.fori_loop(0, order_ref.shape[0], body, 0, unroll=8)


def fetch(pairs, sems):
    copies = [
        pltpu.make_async_copy(source, target, sems.at[i])
        for i, (source, target) in enumerate(pairs)
    ]
    for copy in copies:
        copy.start()
    return copies


def tile_copy(tiles_hbm, tiles_vmem, sems, chunk):
    window = pl.ds(chunk * CHUNK, CHUNK)
    return pltpu.make_async_copy(tiles_hbm.at[window], tiles_vmem.at[window], sems.at[chunk])


def forward_kernel(
    order_hbm,
    rows_hbm,
    cols_hbm,
    count_hbm,
    feats_hbm,
    tiles_hbm,
    partial_ref,
    tiles_ref,
    order_ref,
    rows_ref,
    cols_ref,
    count_ref,
    feats_ref,
    places,
    acc,
    small_sems,
    sems,
):
    slots, tile_size, _ = tiles_ref.shape
    blocks_total, slice_width, _ = partial_ref.shape
    small = fetch(
        [
            (order_hbm, order_ref),
            (rows_hbm, rows_ref),
            (cols_hbm, cols_ref),
            (count_hbm, count_ref),
            (feats_hbm, feats_ref),
        ],
        small_sems,
    )
    for chunk in range(slots // CHUNK):
        tile_copy(tiles_hbm, tiles_ref, sems, chunk).start()
    acc[...] = jnp.zeros_like(acc)
    for copy in small:
        copy.wait()
    invert_order(order_ref, places)
    count = count_ref[0]

    for first in range(0, slots, STACK):
        if first % CHUNK == 0:
            tile_copy(tiles_hbm, tiles_ref, sems, first // CHUNK).wait()
        group = range(first, first + STACK)
        starts = [pl.multiple_of(cols_ref[slot] * tile_size, tile_size) for slot in group]
        stacked = jnp.concatenate(
            [feats_ref[:, pl.ds(start, tile_size)] for start in starts], axis=0
        )
        crossed = lax.dot_general(
            stacked,
            tiles_ref[pl.ds(first, STACK)].reshape(STACK * tile_size, tile_size),
            (((1,), (1,)), ((), ())),
            preferred_element_type=jnp.float32,
        )
        for i, slot in enumerate(group):
            target = jnp.where(slot < count, places[rows_ref[slot]], blocks_total)
            acc[target] += crossed[
                i * slice_width : (i + 1) * slice_width, i * tile_size : (i + 1) * tile_size
            ]

    partial_ref[...] = acc[:blocks_total].astype(partial_ref.dtype)


def dense_kernel(
    got_ref,
    self_ref,
    degree_ref,
    w_self_ref,
    w_neigh_ref,
    bias_ref,
    upstream_ref,
    hidden_ref,
    back_ref,
    summed,
):
    nfeat, ncol, slice_width, tile_size = got_ref.shape
    for f in range(nfeat):
        summed[pl.ds(f * slice_width, slice_width), :] = jnp.sum(
            got_ref[f].astype(jnp.float32), axis=0
        )
    scale = lax.rsqrt(degree_ref[...].astype(jnp.float32))
    aggregate = (summed[...] * scale).astype(jnp.bfloat16)
    pre = jnp.dot(self_ref[...], w_self_ref[...], preferred_element_type=jnp.float32)
    pre = pre + lax.dot_general(
        aggregate, w_neigh_ref[...], (((0,), (0,)), ((), ())), preferred_element_type=jnp.float32
    )
    pre = pre + bias_ref[...]
    gate = jax.nn.sigmoid(pre)
    hidden_ref[...] = (pre * gate).astype(jnp.bfloat16)
    slope = gate * (1.0 + pre * (1.0 - gate))
    dpre = (upstream_ref[...].astype(jnp.float32) * slope).astype(jnp.bfloat16)
    dagg = lax.dot_general(
        w_neigh_ref[...], dpre, (((1,), (1,)), ((), ())), preferred_element_type=jnp.float32
    )
    back = dagg * scale
    for f in range(nfeat):
        piece = back[f * slice_width : (f + 1) * slice_width].astype(jnp.bfloat16)
        for c in range(ncol):
            back_ref[f, c] = piece


def backward_kernel(
    order_hbm,
    rows_hbm,
    cols_hbm,
    count_hbm,
    grads_ref,
    tiles_ref,
    out_ref,
    order_ref,
    rows_ref,
    cols_ref,
    count_ref,
    places,
    acc_even,
    acc_odd,
    small_sems,
):
    slots, tile_size, _ = tiles_ref.shape
    slice_width = out_ref.shape[0]
    small = fetch(
        [
            (order_hbm, order_ref),
            (rows_hbm, rows_ref),
            (cols_hbm, cols_ref),
            (count_hbm, count_ref),
        ],
        small_sems,
    )
    accs = (acc_even, acc_odd)
    for acc in accs:
        acc[...] = jnp.zeros_like(acc)
    for copy in small:
        copy.wait()
    invert_order(order_ref, places)
    col_blocks = out_ref.shape[1] // tile_size
    count = count_ref[0]
    blank = jnp.zeros((slice_width, tile_size), grads_ref.dtype)

    for first in range(0, slots, 2):
        even = grads_ref[places[rows_ref[first]]]
        odd = grads_ref[places[rows_ref[first + 1]]]
        diagonal = jnp.concatenate(
            [
                jnp.concatenate([even, blank], axis=1),
                jnp.concatenate([blank, odd], axis=1),
            ],
            axis=0,
        )
        pieces = jnp.dot(
            diagonal,
            tiles_ref[pl.ds(first, 2)].reshape(2 * tile_size, tile_size),
            preferred_element_type=jnp.float32,
        )
        for i, acc in enumerate(accs):
            target = jnp.where(first + i < count, cols_ref[first + i], col_blocks)
            acc[target] += pieces[i * slice_width : (i + 1) * slice_width]

    for block in range(col_blocks):
        total = acc_even[block] + acc_odd[block]
        out_ref[:, block * tile_size : (block + 1) * tile_size] = total.astype(out_ref.dtype)


VMEM = pl.BlockSpec(memory_space=pltpu.VMEM)
ANY = pl.BlockSpec(memory_space=pl.ANY)


def in_hbm(x):
    return pltpu.with_memory_space_constraint(x, pltpu.HBM)


def local(
    self_feats,
    neighbour_feats,
    tiles,
    tile_rows,
    tile_cols,
    tile_count,
    owner_order,
    degree,
    w_self,
    w_neigh,
    bias,
    upstream,
):
    nfeat = lax.axis_size("feat")
    ncol = lax.axis_size("col")
    slots, tile_size, _ = tiles.shape
    slice_width, width = neighbour_feats.shape
    col_blocks = width // tile_size
    rows = self_feats.shape[0]
    blocks_total = owner_order.shape[0]
    assert rows == tile_size and blocks_total == nfeat * ncol
    index_arrays = [in_hbm(x) for x in (owner_order, tile_rows, tile_cols)] + [tile_count]
    index_scratch = [pltpu.SMEM(x.shape, x.dtype) for x in index_arrays]
    params = pltpu.CompilerParams(vmem_limit_bytes=32 << 20)

    partial_value, tiles_kept = pl.pallas_call(
        forward_kernel,
        out_shape=(
            jax.ShapeDtypeStruct((blocks_total, slice_width, tile_size), jnp.bfloat16),
            pltpu.VMEM(tiles.shape, tiles.dtype),
        ),
        in_specs=[ANY] * 6,
        out_specs=(VMEM, VMEM),
        scratch_shapes=index_scratch
        + [
            pltpu.VMEM(neighbour_feats.shape, neighbour_feats.dtype),
            pltpu.SMEM((blocks_total,), jnp.int32),
            pltpu.VMEM((blocks_total + 1, slice_width, tile_size), jnp.float32),
            pltpu.SemaphoreType.DMA((5,)),
            pltpu.SemaphoreType.DMA((slots // CHUNK,)),
        ],
        compiler_params=params,
        name="forward",
    )(*index_arrays, in_hbm(neighbour_feats), in_hbm(tiles))

    got = lax.all_to_all(partial_value, ("feat", "col"), split_axis=0, concat_axis=0, tiled=True)

    hidden_out, back = pl.pallas_call(
        dense_kernel,
        out_shape=(
            jax.ShapeDtypeStruct(upstream.shape, jnp.bfloat16),
            jax.ShapeDtypeStruct((nfeat, ncol, slice_width, tile_size), jnp.bfloat16),
        ),
        in_specs=[VMEM] * 7,
        out_specs=(VMEM, VMEM),
        scratch_shapes=[pltpu.VMEM((nfeat * slice_width, tile_size), jnp.float32)],
        compiler_params=params,
        name="dense",
    )(
        got.reshape(nfeat, ncol, slice_width, tile_size),
        self_feats,
        degree.reshape(1, rows),
        w_self,
        w_neigh,
        bias.reshape(1, -1),
        upstream,
    )

    row_grads = lax.all_to_all(
        back.reshape(blocks_total, slice_width, tile_size),
        ("feat", "col"),
        split_axis=0,
        concat_axis=0,
        tiled=True,
    )

    neigh_grad = pl.pallas_call(
        backward_kernel,
        out_shape=jax.ShapeDtypeStruct(neighbour_feats.shape, jnp.bfloat16),
        in_specs=[ANY] * 4 + [VMEM] * 2,
        out_specs=VMEM,
        scratch_shapes=index_scratch
        + [
            pltpu.SMEM((blocks_total,), jnp.int32),
            pltpu.VMEM((col_blocks + 1, slice_width, tile_size), jnp.float32),
            pltpu.VMEM((col_blocks + 1, slice_width, tile_size), jnp.float32),
            pltpu.SemaphoreType.DMA((4,)),
        ],
        compiler_params=params,
        name="backward",
    )(
        *index_arrays,
        row_grads,
        pltpu.with_memory_space_constraint(tiles_kept, pltpu.VMEM),
    )
    return (hidden_out, neigh_grad)


def solution(mesh):
    in_specs = (
        P(("feat", "col"), None),
        P("feat", "col"),
        P("col", None, None),
        P("col"),
        P("col"),
        P("col"),
        P(),
        P(("feat", "col")),
        P(),
        P(),
        P(),
        P(("feat", "col"), None),
    )
    out_specs = (P(("feat", "col"), None), P("feat", "col"))
    return jax.shard_map(local, mesh=mesh, in_specs=in_specs, out_specs=out_specs, check_vma=False)
```

```python
import jax
import jax.numpy as jnp
from jax import lax
from jax.experimental import pallas as pl
from jax.experimental.pallas import tpu as pltpu
from jax.sharding import PartitionSpec as P

CHUNK = 64


def invert_order(order_ref, places):
    def body(position, carry):
        places[order_ref[position]] = position
        return carry

    lax.fori_loop(0, order_ref.shape[0], body, 0, unroll=8)


def fetch(pairs, sems):
    copies = [
        pltpu.make_async_copy(source, target, sems.at[i])
        for i, (source, target) in enumerate(pairs)
    ]
    for copy in copies:
        copy.start()
    return copies


def block_diagonal(even, odd):
    blank = jnp.zeros_like(even)
    return jnp.concatenate(
        [jnp.concatenate([even, blank], axis=1), jnp.concatenate([blank, odd], axis=1)], axis=0
    )


def tile_copy(tiles_hbm, tiles_vmem, sems, chunk):
    window = pl.ds(chunk * CHUNK, CHUNK)
    return pltpu.make_async_copy(tiles_hbm.at[window], tiles_vmem.at[window], sems.at[chunk])


def forward_kernel(
    order_hbm,
    rows_hbm,
    cols_hbm,
    count_hbm,
    feats_hbm,
    tiles_hbm,
    partial_ref,
    tiles_ref,
    order_ref,
    rows_ref,
    cols_ref,
    count_ref,
    feats_ref,
    places,
    small_sems,
    sems,
    *accs,
):
    slots, tile_size, _ = tiles_ref.shape
    blocks_total, slice_width, _ = partial_ref.shape
    ncol = len(accs)
    spare = blocks_total // ncol
    small = fetch(
        [
            (order_hbm, order_ref),
            (rows_hbm, rows_ref),
            (cols_hbm, cols_ref),
            (count_hbm, count_ref),
            (feats_hbm, feats_ref),
        ],
        small_sems,
    )
    for chunk in range(slots // CHUNK):
        tile_copy(tiles_hbm, tiles_ref, sems, chunk).start()
    for acc in accs:
        acc[...] = jnp.zeros_like(acc)
    for copy in small:
        copy.wait()
    invert_order(order_ref, places)
    count = count_ref[0]
    zero, one, two = (jnp.asarray(v, tiles_ref.dtype) for v in (0, 1, 2))

    for first in range(0, slots, 2):
        if first % CHUNK == 0:
            tile_copy(tiles_hbm, tiles_ref, sems, first // CHUNK).wait()
        pair = (first, first + 1)
        feats = [
            feats_ref[:, pl.ds(pl.multiple_of(cols_ref[slot] * tile_size, tile_size), tile_size)]
            for slot in pair
        ]
        packed = (tiles_ref[first] + two * tiles_ref[first + 1]).T
        odd = jnp.where(packed >= two, one, zero)
        even = packed - two * odd
        pieces = jnp.dot(
            block_diagonal(*feats),
            jnp.concatenate([even, odd], axis=0),
            preferred_element_type=jnp.float32,
        )
        for i, slot in enumerate(pair):
            target = jnp.where(slot < count, places[rows_ref[slot]] // ncol, spare)
            accs[slot % ncol][target] += pieces[i * slice_width : (i + 1) * slice_width]

    for block in range(blocks_total):
        partial_ref[block] = accs[block % ncol][block // ncol].astype(partial_ref.dtype)


def dense_kernel(
    got_ref,
    self_ref,
    degree_ref,
    w_self_ref,
    w_neigh_ref,
    bias_ref,
    upstream_ref,
    hidden_ref,
    back_ref,
    summed,
):
    nfeat, ncol, slice_width, tile_size = got_ref.shape
    for f in range(nfeat):
        summed[pl.ds(f * slice_width, slice_width), :] = jnp.sum(
            got_ref[f].astype(jnp.float32), axis=0
        )
    scale = lax.rsqrt(degree_ref[...].astype(jnp.float32))
    aggregate = (summed[...] * scale).astype(jnp.bfloat16)
    pre = jnp.dot(self_ref[...], w_self_ref[...], preferred_element_type=jnp.float32)
    pre = pre + lax.dot_general(
        aggregate, w_neigh_ref[...], (((0,), (0,)), ((), ())), preferred_element_type=jnp.float32
    )
    pre = pre + bias_ref[...]
    gate = jax.nn.sigmoid(pre)
    hidden_ref[...] = (pre * gate).astype(jnp.bfloat16)
    slope = gate * (1.0 + pre * (1.0 - gate))
    dpre = (upstream_ref[...].astype(jnp.float32) * slope).astype(jnp.bfloat16)
    dagg = lax.dot_general(
        w_neigh_ref[...], dpre, (((1,), (1,)), ((), ())), preferred_element_type=jnp.float32
    )
    back = dagg * scale
    for f in range(nfeat):
        piece = back[f * slice_width : (f + 1) * slice_width].astype(jnp.bfloat16)
        for c in range(ncol):
            back_ref[f, c] = piece


def backward_kernel(
    order_ref,
    rows_ref,
    cols_ref,
    count_ref,
    grads_ref,
    tiles_ref,
    out_ref,
    places,
    acc_even,
    acc_odd,
):
    slots, tile_size, _ = tiles_ref.shape
    slice_width = out_ref.shape[0]
    invert_order(order_ref, places)
    accs = (acc_even, acc_odd)
    for acc in accs:
        acc[...] = jnp.zeros_like(acc)
    col_blocks = out_ref.shape[1] // tile_size
    count = count_ref[0]

    for first in range(0, slots, 2):
        even = grads_ref[places[rows_ref[first]]]
        odd = grads_ref[places[rows_ref[first + 1]]]
        pieces = jnp.dot(
            block_diagonal(even, odd),
            tiles_ref[pl.ds(first, 2)].reshape(2 * tile_size, tile_size),
            preferred_element_type=jnp.float32,
        )
        for i, acc in enumerate(accs):
            target = jnp.where(first + i < count, cols_ref[first + i], col_blocks)
            acc[target] += pieces[i * slice_width : (i + 1) * slice_width]

    for block in range(col_blocks):
        total = acc_even[block] + acc_odd[block]
        out_ref[:, block * tile_size : (block + 1) * tile_size] = total.astype(out_ref.dtype)


VMEM = pl.BlockSpec(memory_space=pltpu.VMEM)
SMEM = pl.BlockSpec(memory_space=pltpu.SMEM)
ANY = pl.BlockSpec(memory_space=pl.ANY)


def in_hbm(x):
    return pltpu.with_memory_space_constraint(x, pltpu.HBM)


def local(
    self_feats,
    neighbour_feats,
    tiles,
    tile_rows,
    tile_cols,
    tile_count,
    owner_order,
    degree,
    w_self,
    w_neigh,
    bias,
    upstream,
):
    nfeat = lax.axis_size("feat")
    ncol = lax.axis_size("col")
    slots, tile_size, _ = tiles.shape
    slice_width, width = neighbour_feats.shape
    col_blocks = width // tile_size
    rows = self_feats.shape[0]
    blocks_total = owner_order.shape[0]
    assert rows == tile_size and blocks_total == nfeat * ncol
    index_arrays = [in_hbm(x) for x in (owner_order, tile_rows, tile_cols)] + [tile_count]
    index_scratch = [pltpu.SMEM(x.shape, x.dtype) for x in index_arrays]
    params = pltpu.CompilerParams(vmem_limit_bytes=32 << 20)

    partial_value, tiles_kept = pl.pallas_call(
        forward_kernel,
        out_shape=(
            jax.ShapeDtypeStruct((blocks_total, slice_width, tile_size), jnp.bfloat16),
            pltpu.VMEM(tiles.shape, tiles.dtype),
        ),
        in_specs=[ANY] * 6,
        out_specs=(VMEM, VMEM),
        scratch_shapes=index_scratch
        + [
            pltpu.VMEM(neighbour_feats.shape, neighbour_feats.dtype),
            pltpu.SMEM((blocks_total,), jnp.int32),
            pltpu.SemaphoreType.DMA((5,)),
            pltpu.SemaphoreType.DMA((slots // CHUNK,)),
        ]
        + [pltpu.VMEM((blocks_total // ncol + 1, slice_width, tile_size), jnp.float32)] * ncol,
        compiler_params=params,
        name="forward",
    )(*index_arrays, in_hbm(neighbour_feats), in_hbm(tiles))

    got = lax.all_to_all(partial_value, ("feat", "col"), split_axis=0, concat_axis=0, tiled=True)

    hidden_out, back = pl.pallas_call(
        dense_kernel,
        out_shape=(
            jax.ShapeDtypeStruct(upstream.shape, jnp.bfloat16),
            jax.ShapeDtypeStruct((nfeat, ncol, slice_width, tile_size), jnp.bfloat16),
        ),
        in_specs=[VMEM] * 7,
        out_specs=(VMEM, VMEM),
        scratch_shapes=[pltpu.VMEM((nfeat * slice_width, tile_size), jnp.float32)],
        compiler_params=params,
        name="dense",
    )(
        got.reshape(nfeat, ncol, slice_width, tile_size),
        self_feats,
        degree.reshape(1, rows),
        w_self,
        w_neigh,
        bias.reshape(1, -1),
        upstream,
    )

    row_grads = lax.all_to_all(
        back.reshape(blocks_total, slice_width, tile_size),
        ("feat", "col"),
        split_axis=0,
        concat_axis=0,
        tiled=True,
    )

    neigh_grad = pl.pallas_call(
        backward_kernel,
        out_shape=jax.ShapeDtypeStruct(neighbour_feats.shape, jnp.bfloat16),
        in_specs=[SMEM] * 4 + [VMEM] * 2,
        out_specs=VMEM,
        scratch_shapes=[
            pltpu.SMEM((blocks_total,), jnp.int32),
            pltpu.VMEM((col_blocks + 1, slice_width, tile_size), jnp.float32),
            pltpu.VMEM((col_blocks + 1, slice_width, tile_size), jnp.float32),
        ],
        compiler_params=params,
        name="backward",
    )(
        owner_order,
        tile_rows,
        tile_cols,
        tile_count,
        row_grads,
        pltpu.with_memory_space_constraint(tiles_kept, pltpu.VMEM),
    )
    return (hidden_out, neigh_grad)


def solution(mesh):
    in_specs = (
        P(("feat", "col"), None),
        P("feat", "col"),
        P("col", None, None),
        P("col"),
        P("col"),
        P("col"),
        P(),
        P(("feat", "col")),
        P(),
        P(),
        P(),
        P(("feat", "col"), None),
    )
    out_specs = (P(("feat", "col"), None), P("feat", "col"))
    return jax.shard_map(local, mesh=mesh, in_specs=in_specs, out_specs=out_specs, check_vma=False)
```

```python
import jax
import jax.numpy as jnp
from jax import lax
from jax.experimental import pallas as pl
from jax.experimental.pallas import tpu as pltpu
from jax.sharding import PartitionSpec as P

CHUNK = 64


def invert_order(order_ref, places):
    def body(position, carry):
        places[order_ref[position]] = position
        return carry

    lax.fori_loop(0, order_ref.shape[0], body, 0, unroll=8)


def fetch(pairs, sems):
    copies = [
        pltpu.make_async_copy(source, target, sems.at[i])
        for i, (source, target) in enumerate(pairs)
    ]
    for copy in copies:
        copy.start()
    return copies


def block_diagonal(even, odd):
    blank = jnp.zeros_like(even)
    return jnp.concatenate(
        [jnp.concatenate([even, blank], axis=1), jnp.concatenate([blank, odd], axis=1)], axis=0
    )


def tile_copy(tiles_hbm, tiles_vmem, sems, chunk):
    window = pl.ds(chunk * CHUNK, CHUNK)
    return pltpu.make_async_copy(tiles_hbm.at[window], tiles_vmem.at[window], sems.at[chunk])


def forward_kernel(
    order_hbm,
    rows_hbm,
    cols_hbm,
    count_hbm,
    feats_ref,
    tiles_hbm,
    partial_ref,
    tiles_ref,
    order_ref,
    rows_ref,
    cols_ref,
    count_ref,
    places,
    small_sems,
    sems,
    *accs,
):
    slots, tile_size, _ = tiles_ref.shape
    blocks_total, slice_width, _ = partial_ref.shape
    ncol = len(accs)
    spare = blocks_total // ncol
    small = fetch(
        [
            (order_hbm, order_ref),
            (rows_hbm, rows_ref),
            (cols_hbm, cols_ref),
            (count_hbm, count_ref),
        ],
        small_sems,
    )
    for chunk in range(slots // CHUNK):
        tile_copy(tiles_hbm, tiles_ref, sems, chunk).start()
    for acc in accs:
        acc[...] = jnp.zeros_like(acc)
    for copy in small:
        copy.wait()
    invert_order(order_ref, places)
    count = count_ref[0]
    zero, one, two = (jnp.asarray(v, tiles_ref.dtype) for v in (0, 1, 2))

    for first in range(0, slots, 2):
        if first % CHUNK == 0:
            tile_copy(tiles_hbm, tiles_ref, sems, first // CHUNK).wait()
        pair = (first, first + 1)
        feats = [
            feats_ref[:, pl.ds(pl.multiple_of(cols_ref[slot] * tile_size, tile_size), tile_size)]
            for slot in pair
        ]
        packed = (tiles_ref[first] + two * tiles_ref[first + 1]).T
        odd = jnp.where(packed >= two, one, zero)
        even = packed - two * odd
        pieces = jnp.dot(
            block_diagonal(*feats),
            jnp.concatenate([even, odd], axis=0),
            preferred_element_type=jnp.float32,
        )
        for i, slot in enumerate(pair):
            target = jnp.where(slot < count, places[rows_ref[slot]] // ncol, spare)
            accs[slot % ncol][target] += pieces[i * slice_width : (i + 1) * slice_width]

    for block in range(blocks_total):
        partial_ref[block] = accs[block % ncol][block // ncol].astype(partial_ref.dtype)


def dense_kernel(
    got_ref,
    self_ref,
    degree_ref,
    w_self_ref,
    w_neigh_ref,
    bias_ref,
    upstream_ref,
    hidden_ref,
    back_ref,
    summed,
):
    nfeat, ncol, slice_width, tile_size = got_ref.shape
    for f in range(nfeat):
        summed[pl.ds(f * slice_width, slice_width), :] = jnp.sum(
            got_ref[f].astype(jnp.float32), axis=0
        )
    scale = lax.rsqrt(degree_ref[...].astype(jnp.float32))
    aggregate = (summed[...] * scale).astype(jnp.bfloat16)
    pre = jnp.dot(self_ref[...], w_self_ref[...], preferred_element_type=jnp.float32)
    pre = pre + lax.dot_general(
        aggregate, w_neigh_ref[...], (((0,), (0,)), ((), ())), preferred_element_type=jnp.float32
    )
    pre = pre + bias_ref[...]
    gate = jax.nn.sigmoid(pre)
    hidden_ref[...] = (pre * gate).astype(jnp.bfloat16)
    slope = gate * (1.0 + pre * (1.0 - gate))
    dpre = (upstream_ref[...].astype(jnp.float32) * slope).astype(jnp.bfloat16)
    dagg = lax.dot_general(
        w_neigh_ref[...], dpre, (((1,), (1,)), ((), ())), preferred_element_type=jnp.float32
    )
    back = dagg * scale
    for f in range(nfeat):
        piece = back[f * slice_width : (f + 1) * slice_width].astype(jnp.bfloat16)
        for c in range(ncol):
            back_ref[f, c] = piece


def backward_kernel(
    order_ref,
    rows_ref,
    cols_ref,
    count_ref,
    grads_ref,
    tiles_ref,
    out_ref,
    places,
    acc_even,
    acc_odd,
):
    slots, tile_size, _ = tiles_ref.shape
    slice_width = out_ref.shape[0]
    invert_order(order_ref, places)
    accs = (acc_even, acc_odd)
    for acc in accs:
        acc[...] = jnp.zeros_like(acc)
    col_blocks = out_ref.shape[1] // tile_size
    count = count_ref[0]

    for first in range(0, slots, 2):
        even = grads_ref[places[rows_ref[first]]]
        odd = grads_ref[places[rows_ref[first + 1]]]
        pieces = jnp.dot(
            block_diagonal(even, odd),
            tiles_ref[pl.ds(first, 2)].reshape(2 * tile_size, tile_size),
            preferred_element_type=jnp.float32,
        )
        for i, acc in enumerate(accs):
            target = jnp.where(first + i < count, cols_ref[first + i], col_blocks)
            acc[target] += pieces[i * slice_width : (i + 1) * slice_width]

    for block in range(col_blocks):
        total = acc_even[block] + acc_odd[block]
        out_ref[:, block * tile_size : (block + 1) * tile_size] = total.astype(out_ref.dtype)


VMEM = pl.BlockSpec(memory_space=pltpu.VMEM)
SMEM = pl.BlockSpec(memory_space=pltpu.SMEM)
ANY = pl.BlockSpec(memory_space=pl.ANY)


def in_hbm(x):
    return pltpu.with_memory_space_constraint(x, pltpu.HBM)


def local(
    self_feats,
    neighbour_feats,
    tiles,
    tile_rows,
    tile_cols,
    tile_count,
    owner_order,
    degree,
    w_self,
    w_neigh,
    bias,
    upstream,
):
    nfeat = lax.axis_size("feat")
    ncol = lax.axis_size("col")
    slots, tile_size, _ = tiles.shape
    slice_width, width = neighbour_feats.shape
    col_blocks = width // tile_size
    rows = self_feats.shape[0]
    blocks_total = owner_order.shape[0]
    assert rows == tile_size and blocks_total == nfeat * ncol
    index_arrays = [in_hbm(x) for x in (owner_order, tile_rows, tile_cols)] + [tile_count]
    index_scratch = [pltpu.SMEM(x.shape, x.dtype) for x in index_arrays]
    params = pltpu.CompilerParams(vmem_limit_bytes=32 << 20)

    partial_value, tiles_kept = pl.pallas_call(
        forward_kernel,
        out_shape=(
            jax.ShapeDtypeStruct((blocks_total, slice_width, tile_size), jnp.bfloat16),
            pltpu.VMEM(tiles.shape, tiles.dtype),
        ),
        in_specs=[ANY] * 4 + [VMEM, ANY],
        out_specs=(VMEM, VMEM),
        scratch_shapes=index_scratch
        + [
            pltpu.SMEM((blocks_total,), jnp.int32),
            pltpu.SemaphoreType.DMA((4,)),
            pltpu.SemaphoreType.DMA((slots // CHUNK,)),
        ]
        + [pltpu.VMEM((blocks_total // ncol + 1, slice_width, tile_size), jnp.float32)] * ncol,
        compiler_params=params,
        name="forward",
    )(
        *index_arrays,
        pltpu.with_memory_space_constraint(neighbour_feats, pltpu.VMEM),
        in_hbm(tiles),
    )

    got = lax.all_to_all(partial_value, ("feat", "col"), split_axis=0, concat_axis=0, tiled=True)

    hidden_out, back = pl.pallas_call(
        dense_kernel,
        out_shape=(
            jax.ShapeDtypeStruct(upstream.shape, jnp.bfloat16),
            jax.ShapeDtypeStruct((nfeat, ncol, slice_width, tile_size), jnp.bfloat16),
        ),
        in_specs=[VMEM] * 7,
        out_specs=(VMEM, VMEM),
        scratch_shapes=[pltpu.VMEM((nfeat * slice_width, tile_size), jnp.float32)],
        compiler_params=params,
        name="dense",
    )(
        got.reshape(nfeat, ncol, slice_width, tile_size),
        self_feats,
        degree.reshape(1, rows),
        w_self,
        w_neigh,
        bias.reshape(1, -1),
        upstream,
    )

    row_grads = lax.all_to_all(
        back.reshape(blocks_total, slice_width, tile_size),
        ("feat", "col"),
        split_axis=0,
        concat_axis=0,
        tiled=True,
    )

    neigh_grad = pl.pallas_call(
        backward_kernel,
        out_shape=jax.ShapeDtypeStruct(neighbour_feats.shape, jnp.bfloat16),
        in_specs=[SMEM] * 4 + [VMEM] * 2,
        out_specs=VMEM,
        scratch_shapes=[
            pltpu.SMEM((blocks_total,), jnp.int32),
            pltpu.VMEM((col_blocks + 1, slice_width, tile_size), jnp.float32),
            pltpu.VMEM((col_blocks + 1, slice_width, tile_size), jnp.float32),
        ],
        compiler_params=params,
        name="backward",
    )(
        owner_order,
        tile_rows,
        tile_cols,
        tile_count,
        row_grads,
        pltpu.with_memory_space_constraint(tiles_kept, pltpu.VMEM),
    )
    return (hidden_out, neigh_grad)


def solution(mesh):
    in_specs = (
        P(("feat", "col"), None),
        P("feat", "col"),
        P("col", None, None),
        P("col"),
        P("col"),
        P("col"),
        P(),
        P(("feat", "col")),
        P(),
        P(),
        P(),
        P(("feat", "col"), None),
    )
    out_specs = (P(("feat", "col"), None), P("feat", "col"))
    return jax.shard_map(local, mesh=mesh, in_specs=in_specs, out_specs=out_specs, check_vma=False)
```

```python
import jax
import jax.numpy as jnp
from jax import lax
from jax.experimental import pallas as pl
from jax.experimental.pallas import tpu as pltpu
from jax.sharding import PartitionSpec as P

CHUNK = 64


def invert_order(order_ref, places):
    def body(position, carry):
        places[order_ref[position]] = position
        return carry

    lax.fori_loop(0, order_ref.shape[0], body, 0, unroll=8)


def fetch(pairs, sems):
    copies = [
        pltpu.make_async_copy(source, target, sems.at[i])
        for i, (source, target) in enumerate(pairs)
    ]
    for copy in copies:
        copy.start()
    return copies


def block_diagonal(even, odd):
    blank = jnp.zeros_like(even)
    return jnp.concatenate(
        [jnp.concatenate([even, blank], axis=1), jnp.concatenate([blank, odd], axis=1)], axis=0
    )


def tile_copy(tiles_hbm, tiles_vmem, sems, chunk):
    window = pl.ds(chunk * CHUNK, CHUNK)
    return pltpu.make_async_copy(tiles_hbm.at[window], tiles_vmem.at[window], sems.at[chunk])


def forward_kernel(
    order_hbm,
    rows_hbm,
    cols_hbm,
    count_hbm,
    feats_hbm,
    tiles_hbm,
    partial_ref,
    tiles_ref,
    order_ref,
    rows_ref,
    cols_ref,
    count_ref,
    feats_ref,
    feat_blocks,
    places,
    small_sems,
    sems,
    *accs,
):
    slots, tile_size, _ = tiles_ref.shape
    blocks_total, slice_width, _ = partial_ref.shape
    ncol = len(accs)
    spare = blocks_total // ncol
    small = fetch(
        [
            (order_hbm, order_ref),
            (rows_hbm, rows_ref),
            (cols_hbm, cols_ref),
            (count_hbm, count_ref),
            (feats_hbm, feats_ref),
        ],
        small_sems,
    )
    for chunk in range(slots // CHUNK):
        tile_copy(tiles_hbm, tiles_ref, sems, chunk).start(priority=1)
    for acc in accs:
        acc[...] = jnp.zeros_like(acc)
    for copy in small:
        copy.wait()
    for block in range(feat_blocks.shape[0]):
        feat_blocks[block] = feats_ref[:, block * tile_size : (block + 1) * tile_size]
    invert_order(order_ref, places)
    count = count_ref[0]
    zero, one, two = (jnp.asarray(v, tiles_ref.dtype) for v in (0, 1, 2))

    for first in range(0, slots, 2):
        if first % CHUNK == 0:
            tile_copy(tiles_hbm, tiles_ref, sems, first // CHUNK).wait()
        pair = (first, first + 1)
        feats = [feat_blocks[cols_ref[slot]] for slot in pair]
        packed = (tiles_ref[first] + two * tiles_ref[first + 1]).T
        odd = jnp.where(packed >= two, one, zero)
        even = packed - two * odd
        pieces = jnp.dot(
            block_diagonal(*feats),
            jnp.concatenate([even, odd], axis=0),
            preferred_element_type=jnp.float32,
        )
        for i, slot in enumerate(pair):
            target = jnp.where(slot < count, places[rows_ref[slot]] // ncol, spare)
            accs[slot % ncol][target] += pieces[i * slice_width : (i + 1) * slice_width]

    for block in range(blocks_total):
        partial_ref[block] = accs[block % ncol][block // ncol].astype(partial_ref.dtype)


def dense_kernel(
    got_ref,
    self_ref,
    degree_ref,
    w_self_ref,
    w_neigh_ref,
    bias_ref,
    upstream_ref,
    hidden_ref,
    back_ref,
    summed,
):
    nfeat, ncol, slice_width, tile_size = got_ref.shape
    for f in range(nfeat):
        summed[pl.ds(f * slice_width, slice_width), :] = jnp.sum(
            got_ref[f].astype(jnp.float32), axis=0
        )
    scale = lax.rsqrt(degree_ref[...].astype(jnp.float32))
    aggregate = (summed[...] * scale).astype(jnp.bfloat16)
    pre = jnp.dot(self_ref[...], w_self_ref[...], preferred_element_type=jnp.float32)
    pre = pre + lax.dot_general(
        aggregate, w_neigh_ref[...], (((0,), (0,)), ((), ())), preferred_element_type=jnp.float32
    )
    pre = pre + bias_ref[...]
    gate = jax.nn.sigmoid(pre)
    hidden_ref[...] = (pre * gate).astype(jnp.bfloat16)
    slope = gate * (1.0 + pre * (1.0 - gate))
    dpre = (upstream_ref[...].astype(jnp.float32) * slope).astype(jnp.bfloat16)
    dagg = lax.dot_general(
        w_neigh_ref[...], dpre, (((1,), (1,)), ((), ())), preferred_element_type=jnp.float32
    )
    back = dagg * scale
    for f in range(nfeat):
        piece = back[f * slice_width : (f + 1) * slice_width].astype(jnp.bfloat16)
        for c in range(ncol):
            back_ref[f, c] = piece


def backward_kernel(
    order_ref,
    rows_ref,
    cols_ref,
    count_ref,
    grads_ref,
    tiles_ref,
    out_ref,
    places,
    acc_even,
    acc_odd,
):
    slots, tile_size, _ = tiles_ref.shape
    slice_width = out_ref.shape[0]
    invert_order(order_ref, places)
    accs = (acc_even, acc_odd)
    for acc in accs:
        acc[...] = jnp.zeros_like(acc)
    col_blocks = out_ref.shape[1] // tile_size
    count = count_ref[0]

    for first in range(0, slots, 2):
        even = grads_ref[places[rows_ref[first]]]
        odd = grads_ref[places[rows_ref[first + 1]]]
        pieces = jnp.dot(
            block_diagonal(even, odd),
            tiles_ref[pl.ds(first, 2)].reshape(2 * tile_size, tile_size),
            preferred_element_type=jnp.float32,
        )
        for i, acc in enumerate(accs):
            target = jnp.where(first + i < count, cols_ref[first + i], col_blocks)
            acc[target] += pieces[i * slice_width : (i + 1) * slice_width]

    for block in range(col_blocks):
        total = acc_even[block] + acc_odd[block]
        out_ref[:, block * tile_size : (block + 1) * tile_size] = total.astype(out_ref.dtype)


VMEM = pl.BlockSpec(memory_space=pltpu.VMEM)
SMEM = pl.BlockSpec(memory_space=pltpu.SMEM)
ANY = pl.BlockSpec(memory_space=pl.ANY)


def in_hbm(x):
    return pltpu.with_memory_space_constraint(x, pltpu.HBM)


def local(
    self_feats,
    neighbour_feats,
    tiles,
    tile_rows,
    tile_cols,
    tile_count,
    owner_order,
    degree,
    w_self,
    w_neigh,
    bias,
    upstream,
):
    nfeat = lax.axis_size("feat")
    ncol = lax.axis_size("col")
    slots, tile_size, _ = tiles.shape
    slice_width, width = neighbour_feats.shape
    col_blocks = width // tile_size
    rows = self_feats.shape[0]
    blocks_total = owner_order.shape[0]
    assert rows == tile_size and blocks_total == nfeat * ncol
    index_arrays = [in_hbm(x) for x in (owner_order, tile_rows, tile_cols)] + [tile_count]
    index_scratch = [pltpu.SMEM(x.shape, x.dtype) for x in index_arrays]
    params = pltpu.CompilerParams(vmem_limit_bytes=32 << 20)

    partial_value, tiles_kept = pl.pallas_call(
        forward_kernel,
        out_shape=(
            jax.ShapeDtypeStruct((blocks_total, slice_width, tile_size), jnp.bfloat16),
            pltpu.VMEM(tiles.shape, tiles.dtype),
        ),
        in_specs=[ANY] * 6,
        out_specs=(VMEM, VMEM),
        scratch_shapes=index_scratch
        + [
            pltpu.VMEM(neighbour_feats.shape, neighbour_feats.dtype),
            pltpu.VMEM((col_blocks, slice_width, tile_size), neighbour_feats.dtype),
            pltpu.SMEM((blocks_total,), jnp.int32),
            pltpu.SemaphoreType.DMA((5,)),
            pltpu.SemaphoreType.DMA((slots // CHUNK,)),
        ]
        + [pltpu.VMEM((blocks_total // ncol + 1, slice_width, tile_size), jnp.float32)] * ncol,
        compiler_params=params,
        name="forward",
    )(*index_arrays, in_hbm(neighbour_feats), in_hbm(tiles))

    got = lax.all_to_all(partial_value, ("feat", "col"), split_axis=0, concat_axis=0, tiled=True)

    hidden_out, back = pl.pallas_call(
        dense_kernel,
        out_shape=(
            jax.ShapeDtypeStruct(upstream.shape, jnp.bfloat16),
            jax.ShapeDtypeStruct((nfeat, ncol, slice_width, tile_size), jnp.bfloat16),
        ),
        in_specs=[VMEM] * 7,
        out_specs=(VMEM, VMEM),
        scratch_shapes=[pltpu.VMEM((nfeat * slice_width, tile_size), jnp.float32)],
        compiler_params=params,
        name="dense",
    )(
        got.reshape(nfeat, ncol, slice_width, tile_size),
        self_feats,
        degree.reshape(1, rows),
        w_self,
        w_neigh,
        bias.reshape(1, -1),
        upstream,
    )

    row_grads = lax.all_to_all(
        back.reshape(blocks_total, slice_width, tile_size),
        ("feat", "col"),
        split_axis=0,
        concat_axis=0,
        tiled=True,
    )

    neigh_grad = pl.pallas_call(
        backward_kernel,
        out_shape=jax.ShapeDtypeStruct(neighbour_feats.shape, jnp.bfloat16),
        in_specs=[SMEM] * 4 + [VMEM] * 2,
        out_specs=VMEM,
        scratch_shapes=[
            pltpu.SMEM((blocks_total,), jnp.int32),
            pltpu.VMEM((col_blocks + 1, slice_width, tile_size), jnp.float32),
            pltpu.VMEM((col_blocks + 1, slice_width, tile_size), jnp.float32),
        ],
        compiler_params=params,
        name="backward",
    )(
        owner_order,
        tile_rows,
        tile_cols,
        tile_count,
        row_grads,
        pltpu.with_memory_space_constraint(tiles_kept, pltpu.VMEM),
    )
    return (hidden_out, neigh_grad)


def solution(mesh):
    in_specs = (
        P(("feat", "col"), None),
        P("feat", "col"),
        P("col", None, None),
        P("col"),
        P("col"),
        P("col"),
        P(),
        P(("feat", "col")),
        P(),
        P(),
        P(),
        P(("feat", "col"), None),
    )
    out_specs = (P(("feat", "col"), None), P("feat", "col"))
    return jax.shard_map(local, mesh=mesh, in_specs=in_specs, out_specs=out_specs, check_vma=False)
```

```python
import jax
import jax.numpy as jnp
from jax import lax
from jax.experimental import pallas as pl
from jax.experimental.pallas import tpu as pltpu
from jax.sharding import PartitionSpec as P

CHUNK = 64


def invert_order(order_ref, places):
    def body(position, carry):
        places[order_ref[position]] = position
        return carry

    lax.fori_loop(0, order_ref.shape[0], body, 0, unroll=8)


def fetch(pairs, sems):
    copies = [
        pltpu.make_async_copy(source, target, sems.at[i])
        for i, (source, target) in enumerate(pairs)
    ]
    for copy in copies:
        copy.start()
    return copies


def block_diagonal(even, odd):
    blank = jnp.zeros_like(even)
    return jnp.concatenate(
        [jnp.concatenate([even, blank], axis=1), jnp.concatenate([blank, odd], axis=1)], axis=0
    )


def tile_copy(tiles_hbm, tiles_vmem, sems, chunk):
    window = pl.ds(chunk * CHUNK, CHUNK)
    return pltpu.make_async_copy(tiles_hbm.at[window], tiles_vmem.at[window], sems.at[chunk])


def forward_kernel(
    order_hbm,
    rows_hbm,
    cols_hbm,
    count_hbm,
    feats_hbm,
    tiles_hbm,
    partial_ref,
    tiles_ref,
    order_ref,
    rows_ref,
    cols_ref,
    count_ref,
    feats_ref,
    feat_blocks,
    places,
    small_sems,
    sems,
    *accs,
):
    slots, tile_size, _ = tiles_ref.shape
    blocks_total, slice_width, _ = partial_ref.shape
    ncol = len(accs)
    spare = blocks_total // ncol
    small = fetch(
        [
            (order_hbm, order_ref),
            (rows_hbm, rows_ref),
            (cols_hbm, cols_ref),
            (count_hbm, count_ref),
            (feats_hbm, feats_ref),
        ],
        small_sems,
    )
    for chunk in range(slots // CHUNK):
        tile_copy(tiles_hbm, tiles_ref, sems, chunk).start(priority=1)
    for acc in accs:
        acc[...] = jnp.zeros_like(acc)
    for copy in small:
        copy.wait()
    for block in range(feat_blocks.shape[0]):
        feat_blocks[block] = feats_ref[:, block * tile_size : (block + 1) * tile_size]
    invert_order(order_ref, places)
    count = count_ref[0]
    zero, one, two = (jnp.asarray(v, tiles_ref.dtype) for v in (0, 1, 2))

    for first in range(0, slots, 2):
        if first % CHUNK == 0:
            tile_copy(tiles_hbm, tiles_ref, sems, first // CHUNK).wait()
        pair = (first, first + 1)
        feats = [feat_blocks[cols_ref[slot]] for slot in pair]
        packed = (tiles_ref[first] + two * tiles_ref[first + 1]).T
        odd = jnp.where(packed >= two, one, zero)
        even = packed - two * odd
        pieces = jnp.dot(
            block_diagonal(*feats),
            jnp.concatenate([even, odd], axis=0),
            preferred_element_type=jnp.float32,
        )
        for i, slot in enumerate(pair):
            target = jnp.where(slot < count, places[rows_ref[slot]] // ncol, spare)
            accs[slot % ncol][target] += pieces[i * slice_width : (i + 1) * slice_width]

    for block in range(blocks_total):
        partial_ref[block] = accs[block % ncol][block // ncol].astype(partial_ref.dtype)


def dense_kernel(
    got_ref,
    self_ref,
    degree_ref,
    w_self_ref,
    w_neigh_ref,
    bias_ref,
    upstream_ref,
    hidden_ref,
    back_ref,
    summed,
):
    nfeat, ncol, slice_width, tile_size = got_ref.shape
    for f in range(nfeat):
        summed[pl.ds(f * slice_width, slice_width), :] = jnp.sum(
            got_ref[f].astype(jnp.float32), axis=0
        )
    scale = lax.rsqrt(degree_ref[...].astype(jnp.float32))
    aggregate = (summed[...] * scale).astype(jnp.bfloat16)
    pre = jnp.dot(self_ref[...], w_self_ref[...], preferred_element_type=jnp.float32)
    pre = pre + lax.dot_general(
        aggregate, w_neigh_ref[...], (((0,), (0,)), ((), ())), preferred_element_type=jnp.float32
    )
    pre = pre + bias_ref[...]
    gate = jax.nn.sigmoid(pre)
    hidden_ref[...] = (pre * gate).astype(jnp.bfloat16)
    slope = gate * (1.0 + pre * (1.0 - gate))
    dpre = (upstream_ref[...].astype(jnp.float32) * slope).astype(jnp.bfloat16)
    dagg = lax.dot_general(
        w_neigh_ref[...], dpre, (((1,), (1,)), ((), ())), preferred_element_type=jnp.float32
    )
    back = dagg * scale
    for f in range(nfeat):
        piece = back[f * slice_width : (f + 1) * slice_width].astype(jnp.bfloat16)
        for c in range(ncol):
            back_ref[f, c] = piece


def backward_kernel(
    order_ref,
    rows_ref,
    cols_ref,
    count_ref,
    grads_ref,
    tiles_ref,
    hidden_ref,
    out_ref,
    hidden_hbm,
    places,
    acc_even,
    acc_odd,
    hidden_sem,
):
    slots, tile_size, _ = tiles_ref.shape
    slice_width = out_ref.shape[0]
    leaving = pltpu.make_async_copy(hidden_ref, hidden_hbm, hidden_sem)
    leaving.start()
    invert_order(order_ref, places)
    accs = (acc_even, acc_odd)
    for acc in accs:
        acc[...] = jnp.zeros_like(acc)
    col_blocks = out_ref.shape[1] // tile_size
    count = count_ref[0]

    for first in range(0, slots, 2):
        even = grads_ref[places[rows_ref[first]]]
        odd = grads_ref[places[rows_ref[first + 1]]]
        pieces = jnp.dot(
            block_diagonal(even, odd),
            tiles_ref[pl.ds(first, 2)].reshape(2 * tile_size, tile_size),
            preferred_element_type=jnp.float32,
        )
        for i, acc in enumerate(accs):
            target = jnp.where(first + i < count, cols_ref[first + i], col_blocks)
            acc[target] += pieces[i * slice_width : (i + 1) * slice_width]

    for block in range(col_blocks):
        total = acc_even[block] + acc_odd[block]
        out_ref[:, block * tile_size : (block + 1) * tile_size] = total.astype(out_ref.dtype)
    leaving.wait()


VMEM = pl.BlockSpec(memory_space=pltpu.VMEM)
SMEM = pl.BlockSpec(memory_space=pltpu.SMEM)
ANY = pl.BlockSpec(memory_space=pl.ANY)


def in_hbm(x):
    return pltpu.with_memory_space_constraint(x, pltpu.HBM)


def local(
    self_feats,
    neighbour_feats,
    tiles,
    tile_rows,
    tile_cols,
    tile_count,
    owner_order,
    degree,
    w_self,
    w_neigh,
    bias,
    upstream,
):
    nfeat = lax.axis_size("feat")
    ncol = lax.axis_size("col")
    slots, tile_size, _ = tiles.shape
    slice_width, width = neighbour_feats.shape
    col_blocks = width // tile_size
    rows = self_feats.shape[0]
    blocks_total = owner_order.shape[0]
    assert rows == tile_size and blocks_total == nfeat * ncol
    index_arrays = [in_hbm(x) for x in (owner_order, tile_rows, tile_cols)] + [tile_count]
    index_scratch = [pltpu.SMEM(x.shape, x.dtype) for x in index_arrays]
    params = pltpu.CompilerParams(vmem_limit_bytes=32 << 20)

    partial_value, tiles_kept = pl.pallas_call(
        forward_kernel,
        out_shape=(
            jax.ShapeDtypeStruct((blocks_total, slice_width, tile_size), jnp.bfloat16),
            pltpu.VMEM(tiles.shape, tiles.dtype),
        ),
        in_specs=[ANY] * 6,
        out_specs=(VMEM, VMEM),
        scratch_shapes=index_scratch
        + [
            pltpu.VMEM(neighbour_feats.shape, neighbour_feats.dtype),
            pltpu.VMEM((col_blocks, slice_width, tile_size), neighbour_feats.dtype),
            pltpu.SMEM((blocks_total,), jnp.int32),
            pltpu.SemaphoreType.DMA((5,)),
            pltpu.SemaphoreType.DMA((slots // CHUNK,)),
        ]
        + [pltpu.VMEM((blocks_total // ncol + 1, slice_width, tile_size), jnp.float32)] * ncol,
        compiler_params=params,
        name="forward",
    )(*index_arrays, in_hbm(neighbour_feats), in_hbm(tiles))

    got = lax.all_to_all(partial_value, ("feat", "col"), split_axis=0, concat_axis=0, tiled=True)

    hidden, back = pl.pallas_call(
        dense_kernel,
        out_shape=(
            pltpu.VMEM(upstream.shape, jnp.bfloat16),
            jax.ShapeDtypeStruct((nfeat, ncol, slice_width, tile_size), jnp.bfloat16),
        ),
        in_specs=[VMEM] * 7,
        out_specs=(VMEM, VMEM),
        scratch_shapes=[pltpu.VMEM((nfeat * slice_width, tile_size), jnp.float32)],
        compiler_params=params,
        name="dense",
    )(
        got.reshape(nfeat, ncol, slice_width, tile_size),
        self_feats,
        degree.reshape(1, rows),
        w_self,
        w_neigh,
        bias.reshape(1, -1),
        upstream,
    )

    row_grads = lax.all_to_all(
        back.reshape(blocks_total, slice_width, tile_size),
        ("feat", "col"),
        split_axis=0,
        concat_axis=0,
        tiled=True,
    )

    neigh_grad, hidden_out = pl.pallas_call(
        backward_kernel,
        out_shape=(
            jax.ShapeDtypeStruct(neighbour_feats.shape, jnp.bfloat16),
            jax.ShapeDtypeStruct(upstream.shape, jnp.bfloat16),
        ),
        in_specs=[SMEM] * 4 + [VMEM] * 3,
        out_specs=(VMEM, ANY),
        scratch_shapes=[
            pltpu.SMEM((blocks_total,), jnp.int32),
            pltpu.VMEM((col_blocks + 1, slice_width, tile_size), jnp.float32),
            pltpu.VMEM((col_blocks + 1, slice_width, tile_size), jnp.float32),
            pltpu.SemaphoreType.DMA,
        ],
        compiler_params=params,
        name="backward",
    )(
        owner_order,
        tile_rows,
        tile_cols,
        tile_count,
        row_grads,
        pltpu.with_memory_space_constraint(tiles_kept, pltpu.VMEM),
        pltpu.with_memory_space_constraint(hidden, pltpu.VMEM),
    )
    return (hidden_out, neigh_grad)


def solution(mesh):
    in_specs = (
        P(("feat", "col"), None),
        P("feat", "col"),
        P("col", None, None),
        P("col"),
        P("col"),
        P("col"),
        P(),
        P(("feat", "col")),
        P(),
        P(),
        P(),
        P(("feat", "col"), None),
    )
    out_specs = (P(("feat", "col"), None), P("feat", "col"))
    return jax.shard_map(local, mesh=mesh, in_specs=in_specs, out_specs=out_specs, check_vma=False)
```

```python
import functools

import jax
import jax.numpy as jnp
from jax import lax
from jax.experimental import pallas as pl
from jax.experimental.pallas import tpu as pltpu
from jax.sharding import PartitionSpec as P

CHUNK = 64


def invert_order(order_ref, places, value):
    def body(position, carry):
        places[order_ref[position]] = value(position)
        return carry

    lax.fori_loop(0, order_ref.shape[0], body, 0, unroll=8)


def fetch(pairs, sems):
    copies = [
        pltpu.make_async_copy(source, target, sems.at[i])
        for i, (source, target) in enumerate(pairs)
    ]
    for copy in copies:
        copy.start()
    return copies


def block_diagonal(even, odd):
    blank = jnp.zeros_like(even)
    return jnp.concatenate(
        [jnp.concatenate([even, blank], axis=1), jnp.concatenate([blank, odd], axis=1)], axis=0
    )


def tile_copy(tiles_hbm, tiles_vmem, sems, chunk):
    window = pl.ds(chunk * CHUNK, CHUNK)
    return pltpu.make_async_copy(tiles_hbm.at[window], tiles_vmem.at[window], sems.at[chunk])


def forward_kernel(
    order_hbm,
    rows_hbm,
    cols_hbm,
    count_hbm,
    feats_hbm,
    tiles_hbm,
    partial_ref,
    tiles_ref,
    order_ref,
    rows_ref,
    cols_ref,
    count_ref,
    feats_ref,
    feat_blocks,
    places,
    small_sems,
    sems,
    *accs,
):
    slots, tile_size, _ = tiles_ref.shape
    blocks_total, slice_width, _ = partial_ref.shape
    ncol = len(accs)
    nfeat = blocks_total // ncol
    small = fetch(
        [
            (order_hbm, order_ref),
            (rows_hbm, rows_ref),
            (cols_hbm, cols_ref),
            (count_hbm, count_ref),
            (feats_hbm, feats_ref),
        ],
        small_sems,
    )
    for chunk in range(slots // CHUNK):
        tile_copy(tiles_hbm, tiles_ref, sems, chunk).start(priority=1)
    for acc in accs:
        acc[...] = jnp.zeros_like(acc)
    for copy in small:
        copy.wait()
    for block in range(feat_blocks.shape[0]):
        feat_blocks[block] = feats_ref[:, block * tile_size : (block + 1) * tile_size]
    invert_order(order_ref, places, lambda position: position // ncol)
    count = count_ref[0]
    zero, one, two = (jnp.asarray(v, tiles_ref.dtype) for v in (0, 1, 2))

    for first in range(0, slots, 2):
        if first % CHUNK == 0:
            tile_copy(tiles_hbm, tiles_ref, sems, first // CHUNK).wait()
        pair = (first, first + 1)
        feats = [feat_blocks[cols_ref[slot]] for slot in pair]
        packed = (tiles_ref[first] + two * tiles_ref[first + 1]).T
        odd = jnp.where(packed >= two, one, zero)
        even = packed - two * odd
        pieces = jnp.dot(
            block_diagonal(*feats),
            jnp.concatenate([even, odd], axis=0),
            preferred_element_type=jnp.float32,
        )
        for i, slot in enumerate(pair):
            target = jnp.where(slot < count, places[rows_ref[slot]], nfeat)
            accs[slot % ncol][target] += pieces[i * slice_width : (i + 1) * slice_width]

    for col, acc in enumerate(accs):
        partial_ref[col * nfeat : (col + 1) * nfeat] = acc[:nfeat].astype(partial_ref.dtype)


def dense_kernel(
    got_ref,
    self_ref,
    degree_ref,
    w_self_ref,
    w_neigh_ref,
    bias_ref,
    upstream_ref,
    hidden_ref,
    back_ref,
    summed,
):
    ncol, nfeat, slice_width, tile_size = got_ref.shape
    for f in range(nfeat):
        total = got_ref[0, f].astype(jnp.float32)
        for c in range(1, ncol):
            total = total + got_ref[c, f].astype(jnp.float32)
        summed[pl.ds(f * slice_width, slice_width), :] = total
    scale = lax.rsqrt(degree_ref[...].astype(jnp.float32))
    aggregate = (summed[...] * scale).astype(jnp.bfloat16)
    pre = jnp.dot(self_ref[...], w_self_ref[...], preferred_element_type=jnp.float32)
    pre = pre + lax.dot_general(
        aggregate, w_neigh_ref[...], (((0,), (0,)), ((), ())), preferred_element_type=jnp.float32
    )
    pre = pre + bias_ref[...]
    gate = jax.nn.sigmoid(pre)
    hidden_ref[...] = (pre * gate).astype(jnp.bfloat16)
    slope = gate * (1.0 + pre * (1.0 - gate))
    dpre = (upstream_ref[...].astype(jnp.float32) * slope).astype(jnp.bfloat16)
    dagg = lax.dot_general(
        w_neigh_ref[...], dpre, (((1,), (1,)), ((), ())), preferred_element_type=jnp.float32
    )
    back = dagg * scale
    for f in range(nfeat):
        piece = back[f * slice_width : (f + 1) * slice_width].astype(jnp.bfloat16)
        for c in range(ncol):
            back_ref[c, f] = piece


def backward_kernel(
    ncol,
    order_ref,
    rows_ref,
    cols_ref,
    count_ref,
    grads_ref,
    tiles_ref,
    hidden_ref,
    out_ref,
    hidden_hbm,
    places,
    acc_even,
    acc_odd,
    hidden_sem,
):
    slots, tile_size, _ = tiles_ref.shape
    slice_width = out_ref.shape[0]
    nfeat = grads_ref.shape[0] // ncol
    leaving = pltpu.make_async_copy(hidden_ref, hidden_hbm, hidden_sem)
    leaving.start()
    invert_order(
        order_ref, places, lambda position: position % ncol * nfeat + position // ncol
    )
    accs = (acc_even, acc_odd)
    for acc in accs:
        acc[...] = jnp.zeros_like(acc)
    col_blocks = out_ref.shape[1] // tile_size
    count = count_ref[0]

    for first in range(0, slots, 2):
        even = grads_ref[places[rows_ref[first]]]
        odd = grads_ref[places[rows_ref[first + 1]]]
        pieces = jnp.dot(
            block_diagonal(even, odd),
            tiles_ref[pl.ds(first, 2)].reshape(2 * tile_size, tile_size),
            preferred_element_type=jnp.float32,
        )
        for i, acc in enumerate(accs):
            target = jnp.where(first + i < count, cols_ref[first + i], col_blocks)
            acc[target] += pieces[i * slice_width : (i + 1) * slice_width]

    for block in range(col_blocks):
        total = acc_even[block] + acc_odd[block]
        out_ref[:, block * tile_size : (block + 1) * tile_size] = total.astype(out_ref.dtype)
    leaving.wait()


VMEM = pl.BlockSpec(memory_space=pltpu.VMEM)
SMEM = pl.BlockSpec(memory_space=pltpu.SMEM)
ANY = pl.BlockSpec(memory_space=pl.ANY)


def in_hbm(x):
    return pltpu.with_memory_space_constraint(x, pltpu.HBM)


def local(
    self_feats,
    neighbour_feats,
    tiles,
    tile_rows,
    tile_cols,
    tile_count,
    owner_order,
    degree,
    w_self,
    w_neigh,
    bias,
    upstream,
):
    nfeat = lax.axis_size("feat")
    ncol = lax.axis_size("col")
    slots, tile_size, _ = tiles.shape
    slice_width, width = neighbour_feats.shape
    col_blocks = width // tile_size
    rows = self_feats.shape[0]
    blocks_total = owner_order.shape[0]
    assert rows == tile_size and blocks_total == nfeat * ncol
    index_arrays = [in_hbm(x) for x in (owner_order, tile_rows, tile_cols)] + [tile_count]
    index_scratch = [pltpu.SMEM(x.shape, x.dtype) for x in index_arrays]
    params = pltpu.CompilerParams(vmem_limit_bytes=32 << 20)

    partial_value, tiles_kept = pl.pallas_call(
        forward_kernel,
        out_shape=(
            jax.ShapeDtypeStruct((blocks_total, slice_width, tile_size), jnp.bfloat16),
            pltpu.VMEM(tiles.shape, tiles.dtype),
        ),
        in_specs=[ANY] * 6,
        out_specs=(VMEM, VMEM),
        scratch_shapes=index_scratch
        + [
            pltpu.VMEM(neighbour_feats.shape, neighbour_feats.dtype),
            pltpu.VMEM((col_blocks, slice_width, tile_size), neighbour_feats.dtype),
            pltpu.SMEM((blocks_total,), jnp.int32),
            pltpu.SemaphoreType.DMA((5,)),
            pltpu.SemaphoreType.DMA((slots // CHUNK,)),
        ]
        + [pltpu.VMEM((blocks_total // ncol + 1, slice_width, tile_size), jnp.float32)] * ncol,
        compiler_params=params,
        name="forward",
    )(*index_arrays, in_hbm(neighbour_feats), in_hbm(tiles))

    got = lax.all_to_all(partial_value, ("col", "feat"), split_axis=0, concat_axis=0, tiled=True)

    hidden, back = pl.pallas_call(
        dense_kernel,
        out_shape=(
            pltpu.VMEM(upstream.shape, jnp.bfloat16),
            jax.ShapeDtypeStruct((ncol, nfeat, slice_width, tile_size), jnp.bfloat16),
        ),
        in_specs=[VMEM] * 7,
        out_specs=(VMEM, VMEM),
        scratch_shapes=[pltpu.VMEM((nfeat * slice_width, tile_size), jnp.float32)],
        compiler_params=params,
        name="dense",
    )(
        got.reshape(ncol, nfeat, slice_width, tile_size),
        self_feats,
        degree.reshape(1, rows),
        w_self,
        w_neigh,
        bias.reshape(1, -1),
        upstream,
    )

    row_grads = lax.all_to_all(
        back.reshape(blocks_total, slice_width, tile_size),
        ("col", "feat"),
        split_axis=0,
        concat_axis=0,
        tiled=True,
    )

    neigh_grad, hidden_out = pl.pallas_call(
        functools.partial(backward_kernel, ncol),
        out_shape=(
            jax.ShapeDtypeStruct(neighbour_feats.shape, jnp.bfloat16),
            jax.ShapeDtypeStruct(upstream.shape, jnp.bfloat16),
        ),
        in_specs=[SMEM] * 4 + [VMEM] * 3,
        out_specs=(VMEM, ANY),
        scratch_shapes=[
            pltpu.SMEM((blocks_total,), jnp.int32),
            pltpu.VMEM((col_blocks + 1, slice_width, tile_size), jnp.float32),
            pltpu.VMEM((col_blocks + 1, slice_width, tile_size), jnp.float32),
            pltpu.SemaphoreType.DMA,
        ],
        compiler_params=params,
        name="backward",
    )(
        owner_order,
        tile_rows,
        tile_cols,
        tile_count,
        row_grads,
        pltpu.with_memory_space_constraint(tiles_kept, pltpu.VMEM),
        pltpu.with_memory_space_constraint(hidden, pltpu.VMEM),
    )
    return (hidden_out, neigh_grad)


def solution(mesh):
    in_specs = (
        P(("feat", "col"), None),
        P("feat", "col"),
        P("col", None, None),
        P("col"),
        P("col"),
        P("col"),
        P(),
        P(("feat", "col")),
        P(),
        P(),
        P(),
        P(("feat", "col"), None),
    )
    out_specs = (P(("feat", "col"), None), P("feat", "col"))
    return jax.shard_map(local, mesh=mesh, in_specs=in_specs, out_specs=out_specs, check_vma=False)
```

```python
import functools

import jax
import jax.numpy as jnp
from jax import lax
from jax.experimental import pallas as pl
from jax.experimental.pallas import tpu as pltpu
from jax.sharding import PartitionSpec as P

CHUNK = 64


def invert_order(order_ref, places, ncol, value):
    def body(feat, carry):
        for col in range(ncol):
            places[order_ref[feat * ncol + col]] = value(feat, col)
        return carry

    nfeat = order_ref.shape[0] // ncol
    lax.fori_loop(0, nfeat, body, 0, unroll=max(1, 32 // ncol))


def fetch(pairs, sems):
    copies = [
        pltpu.make_async_copy(source, target, sems.at[i])
        for i, (source, target) in enumerate(pairs)
    ]
    for copy in copies:
        copy.start()
    return copies


def block_diagonal(even, odd):
    blank = jnp.zeros_like(even)
    return jnp.concatenate(
        [jnp.concatenate([even, blank], axis=1), jnp.concatenate([blank, odd], axis=1)], axis=0
    )


def tile_copy(tiles_hbm, tiles_vmem, sems, chunk):
    window = pl.ds(chunk * CHUNK, CHUNK)
    return pltpu.make_async_copy(tiles_hbm.at[window], tiles_vmem.at[window], sems.at[chunk])


def forward_kernel(
    order_hbm,
    rows_hbm,
    cols_hbm,
    count_hbm,
    feats_hbm,
    tiles_hbm,
    partial_ref,
    tiles_ref,
    order_ref,
    rows_ref,
    cols_ref,
    count_ref,
    feats_ref,
    feat_blocks,
    places,
    small_sems,
    sems,
    *accs,
):
    slots, tile_size, _ = tiles_ref.shape
    blocks_total, slice_width, _ = partial_ref.shape
    ncol = len(accs)
    nfeat = blocks_total // ncol
    small = fetch(
        [
            (order_hbm, order_ref),
            (rows_hbm, rows_ref),
            (cols_hbm, cols_ref),
            (count_hbm, count_ref),
            (feats_hbm, feats_ref),
        ],
        small_sems,
    )
    for chunk in range(slots // CHUNK):
        tile_copy(tiles_hbm, tiles_ref, sems, chunk).start(priority=1)
    for acc in accs:
        acc[...] = jnp.zeros_like(acc)
    for copy in small:
        copy.wait()
    for block in range(feat_blocks.shape[0]):
        feat_blocks[block] = feats_ref[:, block * tile_size : (block + 1) * tile_size]
    invert_order(order_ref, places, ncol, lambda feat, col: feat)
    count = count_ref[0]
    zero, one, two = (jnp.asarray(v, tiles_ref.dtype) for v in (0, 1, 2))

    for first in range(0, slots, 2):
        if first % CHUNK == 0:
            tile_copy(tiles_hbm, tiles_ref, sems, first // CHUNK).wait()
        pair = (first, first + 1)
        feats = [feat_blocks[cols_ref[slot]] for slot in pair]
        packed = (tiles_ref[first] + two * tiles_ref[first + 1]).T
        odd = jnp.where(packed >= two, one, zero)
        even = packed - two * odd
        pieces = jnp.dot(
            block_diagonal(*feats),
            jnp.concatenate([even, odd], axis=0),
            preferred_element_type=jnp.float32,
        )
        for i, slot in enumerate(pair):
            target = jnp.where(slot < count, places[rows_ref[slot]], nfeat)
            accs[slot % ncol][target] += pieces[i * slice_width : (i + 1) * slice_width]

    for col, acc in enumerate(accs):
        partial_ref[col * nfeat : (col + 1) * nfeat] = acc[:nfeat].astype(partial_ref.dtype)


def dense_kernel(
    got_ref,
    self_ref,
    degree_ref,
    w_self_ref,
    w_neigh_ref,
    bias_ref,
    upstream_ref,
    hidden_ref,
    back_ref,
    summed,
):
    ncol, nfeat, slice_width, tile_size = got_ref.shape
    for f in range(nfeat):
        total = got_ref[0, f].astype(jnp.float32)
        for c in range(1, ncol):
            total = total + got_ref[c, f].astype(jnp.float32)
        summed[pl.ds(f * slice_width, slice_width), :] = total
    scale = lax.rsqrt(degree_ref[...].astype(jnp.float32))
    aggregate = (summed[...] * scale).astype(jnp.bfloat16)
    pre = jnp.dot(self_ref[...], w_self_ref[...], preferred_element_type=jnp.float32)
    pre = pre + lax.dot_general(
        aggregate, w_neigh_ref[...], (((0,), (0,)), ((), ())), preferred_element_type=jnp.float32
    )
    pre = pre + bias_ref[...]
    gate = jax.nn.sigmoid(pre)
    hidden_ref[...] = (pre * gate).astype(jnp.bfloat16)
    slope = gate * (1.0 + pre * (1.0 - gate))
    dpre = (upstream_ref[...].astype(jnp.float32) * slope).astype(jnp.bfloat16)
    dagg = lax.dot_general(
        w_neigh_ref[...], dpre, (((1,), (1,)), ((), ())), preferred_element_type=jnp.float32
    )
    back = dagg * scale
    for f in range(nfeat):
        piece = back[f * slice_width : (f + 1) * slice_width].astype(jnp.bfloat16)
        for c in range(ncol):
            back_ref[c, f] = piece


def backward_kernel(
    ncol,
    order_ref,
    rows_ref,
    cols_ref,
    count_ref,
    grads_ref,
    tiles_ref,
    hidden_ref,
    out_ref,
    hidden_hbm,
    places,
    acc_even,
    acc_odd,
    hidden_sem,
):
    slots, tile_size, _ = tiles_ref.shape
    slice_width = out_ref.shape[0]
    nfeat = grads_ref.shape[0] // ncol
    leaving = pltpu.make_async_copy(hidden_ref, hidden_hbm, hidden_sem)
    leaving.start()
    invert_order(order_ref, places, ncol, lambda feat, col: col * nfeat + feat)
    accs = (acc_even, acc_odd)
    for acc in accs:
        acc[...] = jnp.zeros_like(acc)
    col_blocks = out_ref.shape[1] // tile_size
    count = count_ref[0]

    for first in range(0, slots, 2):
        even = grads_ref[places[rows_ref[first]]]
        odd = grads_ref[places[rows_ref[first + 1]]]
        pieces = jnp.dot(
            block_diagonal(even, odd),
            tiles_ref[pl.ds(first, 2)].reshape(2 * tile_size, tile_size),
            preferred_element_type=jnp.float32,
        )
        for i, acc in enumerate(accs):
            target = jnp.where(first + i < count, cols_ref[first + i], col_blocks)
            acc[target] += pieces[i * slice_width : (i + 1) * slice_width]

    for block in range(col_blocks):
        total = acc_even[block] + acc_odd[block]
        out_ref[:, block * tile_size : (block + 1) * tile_size] = total.astype(out_ref.dtype)
    leaving.wait()


VMEM = pl.BlockSpec(memory_space=pltpu.VMEM)
SMEM = pl.BlockSpec(memory_space=pltpu.SMEM)
ANY = pl.BlockSpec(memory_space=pl.ANY)


def in_hbm(x):
    return pltpu.with_memory_space_constraint(x, pltpu.HBM)


def local(
    self_feats,
    neighbour_feats,
    tiles,
    tile_rows,
    tile_cols,
    tile_count,
    owner_order,
    degree,
    w_self,
    w_neigh,
    bias,
    upstream,
):
    nfeat = lax.axis_size("feat")
    ncol = lax.axis_size("col")
    slots, tile_size, _ = tiles.shape
    slice_width, width = neighbour_feats.shape
    col_blocks = width // tile_size
    rows = self_feats.shape[0]
    blocks_total = owner_order.shape[0]
    assert rows == tile_size and blocks_total == nfeat * ncol
    index_arrays = [in_hbm(x) for x in (owner_order, tile_rows, tile_cols)] + [tile_count]
    index_scratch = [pltpu.SMEM(x.shape, x.dtype) for x in index_arrays]
    params = pltpu.CompilerParams(vmem_limit_bytes=32 << 20)

    partial_value, tiles_kept = pl.pallas_call(
        forward_kernel,
        out_shape=(
            jax.ShapeDtypeStruct((blocks_total, slice_width, tile_size), jnp.bfloat16),
            pltpu.VMEM(tiles.shape, tiles.dtype),
        ),
        in_specs=[ANY] * 6,
        out_specs=(VMEM, VMEM),
        scratch_shapes=index_scratch
        + [
            pltpu.VMEM(neighbour_feats.shape, neighbour_feats.dtype),
            pltpu.VMEM((col_blocks, slice_width, tile_size), neighbour_feats.dtype),
            pltpu.SMEM((blocks_total,), jnp.int32),
            pltpu.SemaphoreType.DMA((5,)),
            pltpu.SemaphoreType.DMA((slots // CHUNK,)),
        ]
        + [pltpu.VMEM((blocks_total // ncol + 1, slice_width, tile_size), jnp.float32)] * ncol,
        compiler_params=params,
        name="forward",
    )(*index_arrays, in_hbm(neighbour_feats), in_hbm(tiles))

    got = lax.all_to_all(partial_value, ("col", "feat"), split_axis=0, concat_axis=0, tiled=True)

    hidden, back = pl.pallas_call(
        dense_kernel,
        out_shape=(
            pltpu.VMEM(upstream.shape, jnp.bfloat16),
            jax.ShapeDtypeStruct((ncol, nfeat, slice_width, tile_size), jnp.bfloat16),
        ),
        in_specs=[VMEM] * 7,
        out_specs=(VMEM, VMEM),
        scratch_shapes=[pltpu.VMEM((nfeat * slice_width, tile_size), jnp.float32)],
        compiler_params=params,
        name="dense",
    )(
        got.reshape(ncol, nfeat, slice_width, tile_size),
        self_feats,
        degree.reshape(1, rows),
        w_self,
        w_neigh,
        bias.reshape(1, -1),
        upstream,
    )

    row_grads = lax.all_to_all(
        back.reshape(blocks_total, slice_width, tile_size),
        ("col", "feat"),
        split_axis=0,
        concat_axis=0,
        tiled=True,
    )

    neigh_grad, hidden_out = pl.pallas_call(
        functools.partial(backward_kernel, ncol),
        out_shape=(
            jax.ShapeDtypeStruct(neighbour_feats.shape, jnp.bfloat16),
            jax.ShapeDtypeStruct(upstream.shape, jnp.bfloat16),
        ),
        in_specs=[SMEM] * 4 + [VMEM] * 3,
        out_specs=(VMEM, ANY),
        scratch_shapes=[
            pltpu.SMEM((blocks_total,), jnp.int32),
            pltpu.VMEM((col_blocks + 1, slice_width, tile_size), jnp.float32),
            pltpu.VMEM((col_blocks + 1, slice_width, tile_size), jnp.float32),
            pltpu.SemaphoreType.DMA,
        ],
        compiler_params=params,
        name="backward",
    )(
        owner_order,
        tile_rows,
        tile_cols,
        tile_count,
        row_grads,
        pltpu.with_memory_space_constraint(tiles_kept, pltpu.VMEM),
        pltpu.with_memory_space_constraint(hidden, pltpu.VMEM),
    )
    return (hidden_out, neigh_grad)


def solution(mesh):
    in_specs = (
        P(("feat", "col"), None),
        P("feat", "col"),
        P("col", None, None),
        P("col"),
        P("col"),
        P("col"),
        P(),
        P(("feat", "col")),
        P(),
        P(),
        P(),
        P(("feat", "col"), None),
    )
    out_specs = (P(("feat", "col"), None), P("feat", "col"))
    return jax.shard_map(local, mesh=mesh, in_specs=in_specs, out_specs=out_specs, check_vma=False)
```

```python
import functools

import jax
import jax.numpy as jnp
from jax import lax
from jax.experimental import pallas as pl
from jax.experimental.pallas import tpu as pltpu
from jax.sharding import PartitionSpec as P

CHUNK = 64


def invert_order(order_ref, places, ncol, value):
    def body(feat, carry):
        for col in range(ncol):
            places[order_ref[feat * ncol + col]] = value(feat, col)
        return carry

    nfeat = order_ref.shape[0] // ncol
    lax.fori_loop(0, nfeat, body, 0, unroll=max(1, 8 // ncol))


def fetch(pairs, sems):
    copies = [
        pltpu.make_async_copy(source, target, sems.at[i])
        for i, (source, target) in enumerate(pairs)
    ]
    for copy in copies:
        copy.start()
    return copies


def block_diagonal(even, odd):
    blank = jnp.zeros_like(even)
    return jnp.concatenate(
        [jnp.concatenate([even, blank], axis=1), jnp.concatenate([blank, odd], axis=1)], axis=0
    )


def tile_copy(tiles_hbm, tiles_vmem, sems, chunk):
    window = pl.ds(chunk * CHUNK, CHUNK)
    return pltpu.make_async_copy(tiles_hbm.at[window], tiles_vmem.at[window], sems.at[chunk])


def forward_kernel(
    order_hbm,
    rows_hbm,
    cols_hbm,
    count_hbm,
    feats_hbm,
    tiles_hbm,
    partial_ref,
    tiles_ref,
    order_ref,
    rows_ref,
    cols_ref,
    count_ref,
    feats_ref,
    feat_blocks,
    places,
    small_sems,
    sems,
    *accs,
):
    slots, tile_size, _ = tiles_ref.shape
    blocks_total, slice_width, _ = partial_ref.shape
    ncol = len(accs)
    nfeat = blocks_total // ncol
    small = fetch(
        [
            (order_hbm, order_ref),
            (rows_hbm, rows_ref),
            (cols_hbm, cols_ref),
            (count_hbm, count_ref),
            (feats_hbm, feats_ref),
        ],
        small_sems,
    )
    for chunk in range(slots // CHUNK):
        tile_copy(tiles_hbm, tiles_ref, sems, chunk).start(priority=1)
    for acc in accs:
        acc[...] = jnp.zeros_like(acc)
    for copy in small:
        copy.wait()
    for block in range(feat_blocks.shape[0]):
        feat_blocks[block] = feats_ref[:, block * tile_size : (block + 1) * tile_size]
    invert_order(order_ref, places, ncol, lambda feat, col: feat)
    count = count_ref[0]
    zero, one, two = (jnp.asarray(v, tiles_ref.dtype) for v in (0, 1, 2))

    for first in range(0, slots, 2):
        if first % CHUNK == 0:
            tile_copy(tiles_hbm, tiles_ref, sems, first // CHUNK).wait()
        pair = (first, first + 1)
        feats = [feat_blocks[cols_ref[slot]] for slot in pair]
        packed = (tiles_ref[first] + two * tiles_ref[first + 1]).T
        odd = jnp.where(packed >= two, one, zero)
        even = packed - two * odd
        pieces = jnp.dot(
            block_diagonal(*feats),
            jnp.concatenate([even, odd], axis=0),
            preferred_element_type=jnp.float32,
        )
        for i, slot in enumerate(pair):
            target = jnp.where(slot < count, places[rows_ref[slot]], nfeat)
            accs[slot % ncol][target] += pieces[i * slice_width : (i + 1) * slice_width]

    for col, acc in enumerate(accs):
        partial_ref[col * nfeat : (col + 1) * nfeat] = acc[:nfeat].astype(partial_ref.dtype)


def dense_kernel(
    got_ref,
    self_ref,
    degree_ref,
    w_self_ref,
    w_neigh_ref,
    bias_ref,
    upstream_ref,
    hidden_ref,
    back_ref,
    summed,
):
    ncol, nfeat, slice_width, tile_size = got_ref.shape
    for f in range(nfeat):
        total = got_ref[0, f].astype(jnp.float32)
        for c in range(1, ncol):
            total = total + got_ref[c, f].astype(jnp.float32)
        summed[pl.ds(f * slice_width, slice_width), :] = total
    scale = lax.rsqrt(degree_ref[...].astype(jnp.float32))
    aggregate = (summed[...] * scale).astype(jnp.bfloat16)
    pre = jnp.dot(self_ref[...], w_self_ref[...], preferred_element_type=jnp.float32)
    pre = pre + lax.dot_general(
        aggregate, w_neigh_ref[...], (((0,), (0,)), ((), ())), preferred_element_type=jnp.float32
    )
    pre = pre + bias_ref[...]
    gate = jax.nn.sigmoid(pre)
    hidden_ref[...] = (pre * gate).astype(jnp.bfloat16)
    slope = gate * (1.0 + pre * (1.0 - gate))
    dpre = (upstream_ref[...].astype(jnp.float32) * slope).astype(jnp.bfloat16)
    dagg = lax.dot_general(
        w_neigh_ref[...], dpre, (((1,), (1,)), ((), ())), preferred_element_type=jnp.float32
    )
    back = dagg * scale
    for f in range(nfeat):
        piece = back[f * slice_width : (f + 1) * slice_width].astype(jnp.bfloat16)
        for c in range(ncol):
            back_ref[c, f] = piece


def backward_kernel(
    ncol,
    order_ref,
    rows_ref,
    cols_ref,
    count_ref,
    grads_ref,
    tiles_ref,
    hidden_ref,
    out_ref,
    hidden_hbm,
    places,
    acc_even,
    acc_odd,
    hidden_sem,
):
    slots, tile_size, _ = tiles_ref.shape
    slice_width = out_ref.shape[0]
    nfeat = grads_ref.shape[0] // ncol
    leaving = pltpu.make_async_copy(hidden_ref, hidden_hbm, hidden_sem)
    leaving.start()
    invert_order(order_ref, places, ncol, lambda feat, col: col * nfeat + feat)
    accs = (acc_even, acc_odd)
    for acc in accs:
        acc[...] = jnp.zeros_like(acc)
    col_blocks = out_ref.shape[1] // tile_size
    count = count_ref[0]

    for first in range(0, slots, 2):
        even = grads_ref[places[rows_ref[first]]]
        odd = grads_ref[places[rows_ref[first + 1]]]
        pieces = jnp.dot(
            block_diagonal(even, odd),
            tiles_ref[pl.ds(first, 2)].reshape(2 * tile_size, tile_size),
            preferred_element_type=jnp.float32,
        )
        for i, acc in enumerate(accs):
            target = jnp.where(first + i < count, cols_ref[first + i], col_blocks)
            acc[target] += pieces[i * slice_width : (i + 1) * slice_width]

    for block in range(col_blocks):
        total = acc_even[block] + acc_odd[block]
        out_ref[:, block * tile_size : (block + 1) * tile_size] = total.astype(out_ref.dtype)
    leaving.wait()


VMEM = pl.BlockSpec(memory_space=pltpu.VMEM)
SMEM = pl.BlockSpec(memory_space=pltpu.SMEM)
ANY = pl.BlockSpec(memory_space=pl.ANY)


def in_hbm(x):
    return pltpu.with_memory_space_constraint(x, pltpu.HBM)


def local(
    self_feats,
    neighbour_feats,
    tiles,
    tile_rows,
    tile_cols,
    tile_count,
    owner_order,
    degree,
    w_self,
    w_neigh,
    bias,
    upstream,
):
    nfeat = lax.axis_size("feat")
    ncol = lax.axis_size("col")
    slots, tile_size, _ = tiles.shape
    slice_width, width = neighbour_feats.shape
    col_blocks = width // tile_size
    rows = self_feats.shape[0]
    blocks_total = owner_order.shape[0]
    assert rows == tile_size and blocks_total == nfeat * ncol
    index_arrays = [in_hbm(x) for x in (owner_order, tile_rows, tile_cols)] + [tile_count]
    index_scratch = [pltpu.SMEM(x.shape, x.dtype) for x in index_arrays]
    params = pltpu.CompilerParams(vmem_limit_bytes=32 << 20)

    partial_value, tiles_kept = pl.pallas_call(
        forward_kernel,
        out_shape=(
            jax.ShapeDtypeStruct((blocks_total, slice_width, tile_size), jnp.bfloat16),
            pltpu.VMEM(tiles.shape, tiles.dtype),
        ),
        in_specs=[ANY] * 6,
        out_specs=(VMEM, VMEM),
        scratch_shapes=index_scratch
        + [
            pltpu.VMEM(neighbour_feats.shape, neighbour_feats.dtype),
            pltpu.VMEM((col_blocks, slice_width, tile_size), neighbour_feats.dtype),
            pltpu.SMEM((blocks_total,), jnp.int32),
            pltpu.SemaphoreType.DMA((5,)),
            pltpu.SemaphoreType.DMA((slots // CHUNK,)),
        ]
        + [pltpu.VMEM((blocks_total // ncol + 1, slice_width, tile_size), jnp.float32)] * ncol,
        compiler_params=params,
        name="forward",
    )(*index_arrays, in_hbm(neighbour_feats), in_hbm(tiles))

    got = lax.all_to_all(partial_value, ("col", "feat"), split_axis=0, concat_axis=0, tiled=True)

    hidden, back = pl.pallas_call(
        dense_kernel,
        out_shape=(
            pltpu.VMEM(upstream.shape, jnp.bfloat16),
            jax.ShapeDtypeStruct((ncol, nfeat, slice_width, tile_size), jnp.bfloat16),
        ),
        in_specs=[VMEM] * 7,
        out_specs=(VMEM, VMEM),
        scratch_shapes=[pltpu.VMEM((nfeat * slice_width, tile_size), jnp.float32)],
        compiler_params=params,
        name="dense",
    )(
        got.reshape(ncol, nfeat, slice_width, tile_size),
        self_feats,
        degree.reshape(1, rows),
        w_self,
        w_neigh,
        bias.reshape(1, -1),
        upstream,
    )

    row_grads = lax.all_to_all(
        back.reshape(blocks_total, slice_width, tile_size),
        ("col", "feat"),
        split_axis=0,
        concat_axis=0,
        tiled=True,
    )

    neigh_grad, hidden_out = pl.pallas_call(
        functools.partial(backward_kernel, ncol),
        out_shape=(
            jax.ShapeDtypeStruct(neighbour_feats.shape, jnp.bfloat16),
            jax.ShapeDtypeStruct(upstream.shape, jnp.bfloat16),
        ),
        in_specs=[SMEM] * 4 + [VMEM] * 3,
        out_specs=(VMEM, ANY),
        scratch_shapes=[
            pltpu.SMEM((blocks_total,), jnp.int32),
            pltpu.VMEM((col_blocks + 1, slice_width, tile_size), jnp.float32),
            pltpu.VMEM((col_blocks + 1, slice_width, tile_size), jnp.float32),
            pltpu.SemaphoreType.DMA,
        ],
        compiler_params=params,
        name="backward",
    )(
        owner_order,
        tile_rows,
        tile_cols,
        tile_count,
        row_grads,
        pltpu.with_memory_space_constraint(tiles_kept, pltpu.VMEM),
        pltpu.with_memory_space_constraint(hidden, pltpu.VMEM),
    )
    return (hidden_out, neigh_grad)


def solution(mesh):
    in_specs = (
        P(("feat", "col"), None),
        P("feat", "col"),
        P("col", None, None),
        P("col"),
        P("col"),
        P("col"),
        P(),
        P(("feat", "col")),
        P(),
        P(),
        P(),
        P(("feat", "col"), None),
    )
    out_specs = (P(("feat", "col"), None), P("feat", "col"))
    return jax.shard_map(local, mesh=mesh, in_specs=in_specs, out_specs=out_specs, check_vma=False)
```

```python
import functools

import jax
import jax.numpy as jnp
from jax import lax
from jax.experimental import pallas as pl
from jax.experimental.pallas import tpu as pltpu
from jax.sharding import PartitionSpec as P

CHUNK = 64


def invert_order(order_ref, places, ncol, value):
    def body(feat, carry):
        for col in range(ncol):
            places[order_ref[feat * ncol + col]] = value(feat, col)
        return carry

    nfeat = order_ref.shape[0] // ncol
    lax.fori_loop(0, nfeat, body, 0, unroll=max(1, 8 // ncol))


def fetch(pairs, sems):
    copies = [
        pltpu.make_async_copy(source, target, sems.at[i])
        for i, (source, target) in enumerate(pairs)
    ]
    for copy in copies:
        copy.start()
    return copies


def block_diagonal(even, odd):
    blank = jnp.zeros_like(even)
    return jnp.concatenate(
        [jnp.concatenate([even, blank], axis=1), jnp.concatenate([blank, odd], axis=1)], axis=0
    )


def tile_copy(tiles_hbm, tiles_vmem, sems, chunk):
    window = pl.ds(chunk * CHUNK, CHUNK)
    return pltpu.make_async_copy(tiles_hbm.at[window], tiles_vmem.at[window], sems.at[chunk])


def forward_kernel(
    order_hbm,
    rows_hbm,
    cols_hbm,
    count_hbm,
    feats_hbm,
    tiles_hbm,
    partial_ref,
    kept_ref,
    order_ref,
    rows_ref,
    cols_ref,
    count_ref,
    feats_ref,
    feat_blocks,
    tiles_ref,
    places,
    small_sems,
    sems,
    *accs,
):
    slots, tile_size, _ = tiles_ref.shape
    blocks_total, slice_width, _ = partial_ref.shape
    ncol = len(accs)
    nfeat = blocks_total // ncol
    small = fetch(
        [
            (order_hbm, order_ref),
            (rows_hbm, rows_ref),
            (cols_hbm, cols_ref),
            (count_hbm, count_ref),
            (feats_hbm, feats_ref),
        ],
        small_sems,
    )
    for chunk in range(slots // CHUNK):
        tile_copy(tiles_hbm, tiles_ref, sems, chunk).start(priority=1)
    for acc in accs:
        acc[...] = jnp.zeros_like(acc)
    for copy in small:
        copy.wait()
    for block in range(feat_blocks.shape[0]):
        feat_blocks[block] = feats_ref[:, block * tile_size : (block + 1) * tile_size]
    invert_order(order_ref, places, ncol, lambda feat, col: feat)
    count = count_ref[0]
    zero, one, two = (jnp.asarray(v, tiles_ref.dtype) for v in (0, 1, 2))

    for first in range(0, slots, 2):
        if first % CHUNK == 0:
            tile_copy(tiles_hbm, tiles_ref, sems, first // CHUNK).wait()
        pair = (first, first + 1)
        kept_ref[pl.ds(first, 2)] = tiles_ref[pl.ds(first, 2)].astype(kept_ref.dtype)
        feats = [feat_blocks[cols_ref[slot]] for slot in pair]
        packed = (tiles_ref[first] + two * tiles_ref[first + 1]).T
        odd = jnp.where(packed >= two, one, zero)
        even = packed - two * odd
        pieces = jnp.dot(
            block_diagonal(*feats),
            jnp.concatenate([even, odd], axis=0),
            preferred_element_type=jnp.float32,
        )
        for i, slot in enumerate(pair):
            target = jnp.where(slot < count, places[rows_ref[slot]], nfeat)
            accs[slot % ncol][target] += pieces[i * slice_width : (i + 1) * slice_width]

    for col, acc in enumerate(accs):
        partial_ref[col * nfeat : (col + 1) * nfeat] = acc[:nfeat].astype(partial_ref.dtype)


def dense_kernel(
    got_ref,
    self_ref,
    degree_ref,
    w_self_ref,
    w_neigh_ref,
    bias_ref,
    upstream_ref,
    hidden_ref,
    back_ref,
    summed,
):
    ncol, nfeat, slice_width, tile_size = got_ref.shape
    for f in range(nfeat):
        total = got_ref[0, f].astype(jnp.float32)
        for c in range(1, ncol):
            total = total + got_ref[c, f].astype(jnp.float32)
        summed[pl.ds(f * slice_width, slice_width), :] = total
    scale = lax.rsqrt(degree_ref[...].astype(jnp.float32))
    aggregate = (summed[...] * scale).astype(jnp.bfloat16)
    pre = jnp.dot(self_ref[...], w_self_ref[...], preferred_element_type=jnp.float32)
    pre = pre + lax.dot_general(
        aggregate, w_neigh_ref[...], (((0,), (0,)), ((), ())), preferred_element_type=jnp.float32
    )
    pre = pre + bias_ref[...]
    gate = jax.nn.sigmoid(pre)
    hidden_ref[...] = (pre * gate).astype(jnp.bfloat16)
    slope = gate * (1.0 + pre * (1.0 - gate))
    dpre = (upstream_ref[...].astype(jnp.float32) * slope).astype(jnp.bfloat16)
    dagg = lax.dot_general(
        w_neigh_ref[...], dpre, (((1,), (1,)), ((), ())), preferred_element_type=jnp.float32
    )
    back = dagg * scale
    for f in range(nfeat):
        piece = back[f * slice_width : (f + 1) * slice_width].astype(jnp.bfloat16)
        for c in range(ncol):
            back_ref[c, f] = piece


def backward_kernel(
    ncol,
    order_ref,
    rows_ref,
    cols_ref,
    count_ref,
    grads_ref,
    tiles_ref,
    hidden_ref,
    out_ref,
    hidden_hbm,
    places,
    acc_even,
    acc_odd,
    hidden_sem,
):
    slots, tile_size, _ = tiles_ref.shape
    slice_width = out_ref.shape[0]
    nfeat = grads_ref.shape[0] // ncol
    leaving = pltpu.make_async_copy(hidden_ref, hidden_hbm, hidden_sem)
    leaving.start()
    invert_order(order_ref, places, ncol, lambda feat, col: col * nfeat + feat)
    accs = (acc_even, acc_odd)
    for acc in accs:
        acc[...] = jnp.zeros_like(acc)
    col_blocks = out_ref.shape[1] // tile_size
    count = count_ref[0]

    for first in range(0, slots, 2):
        even = grads_ref[places[rows_ref[first]]]
        odd = grads_ref[places[rows_ref[first + 1]]]
        pieces = lax.dot_general(
            block_diagonal(even, odd),
            tiles_ref[pl.ds(first, 2)].reshape(2 * tile_size, tile_size),
            (((1,), (0,)), ((), ())),
            preferred_element_type=jnp.float32,
        )
        for i, acc in enumerate(accs):
            target = jnp.where(first + i < count, cols_ref[first + i], col_blocks)
            acc[target] += pieces[i * slice_width : (i + 1) * slice_width]

    for block in range(col_blocks):
        total = acc_even[block] + acc_odd[block]
        out_ref[:, block * tile_size : (block + 1) * tile_size] = total.astype(out_ref.dtype)
    leaving.wait()


VMEM = pl.BlockSpec(memory_space=pltpu.VMEM)
SMEM = pl.BlockSpec(memory_space=pltpu.SMEM)
ANY = pl.BlockSpec(memory_space=pl.ANY)


def in_hbm(x):
    return pltpu.with_memory_space_constraint(x, pltpu.HBM)


def local(
    self_feats,
    neighbour_feats,
    tiles,
    tile_rows,
    tile_cols,
    tile_count,
    owner_order,
    degree,
    w_self,
    w_neigh,
    bias,
    upstream,
):
    nfeat = lax.axis_size("feat")
    ncol = lax.axis_size("col")
    slots, tile_size, _ = tiles.shape
    slice_width, width = neighbour_feats.shape
    col_blocks = width // tile_size
    rows = self_feats.shape[0]
    blocks_total = owner_order.shape[0]
    assert rows == tile_size and blocks_total == nfeat * ncol
    index_arrays = [in_hbm(x) for x in (owner_order, tile_rows, tile_cols)] + [tile_count]
    index_scratch = [pltpu.SMEM(x.shape, x.dtype) for x in index_arrays]
    params = pltpu.CompilerParams(vmem_limit_bytes=32 << 20)

    partial_value, tiles_kept = pl.pallas_call(
        forward_kernel,
        out_shape=(
            jax.ShapeDtypeStruct((blocks_total, slice_width, tile_size), jnp.bfloat16),
            pltpu.VMEM(tiles.shape, jnp.float8_e4m3fn),
        ),
        in_specs=[ANY] * 6,
        out_specs=(VMEM, VMEM),
        scratch_shapes=index_scratch
        + [
            pltpu.VMEM(neighbour_feats.shape, neighbour_feats.dtype),
            pltpu.VMEM((col_blocks, slice_width, tile_size), neighbour_feats.dtype),
            pltpu.VMEM(tiles.shape, tiles.dtype),
            pltpu.SMEM((blocks_total,), jnp.int32),
            pltpu.SemaphoreType.DMA((5,)),
            pltpu.SemaphoreType.DMA((slots // CHUNK,)),
        ]
        + [pltpu.VMEM((blocks_total // ncol + 1, slice_width, tile_size), jnp.float32)] * ncol,
        compiler_params=params,
        name="forward",
    )(*index_arrays, in_hbm(neighbour_feats), in_hbm(tiles))

    got = lax.all_to_all(partial_value, ("col", "feat"), split_axis=0, concat_axis=0, tiled=True)

    hidden, back = pl.pallas_call(
        dense_kernel,
        out_shape=(
            pltpu.VMEM(upstream.shape, jnp.bfloat16),
            jax.ShapeDtypeStruct((ncol, nfeat, slice_width, tile_size), jnp.bfloat16),
        ),
        in_specs=[VMEM] * 7,
        out_specs=(VMEM, VMEM),
        scratch_shapes=[pltpu.VMEM((nfeat * slice_width, tile_size), jnp.float32)],
        compiler_params=params,
        name="dense",
    )(
        got.reshape(ncol, nfeat, slice_width, tile_size),
        self_feats,
        degree.reshape(1, rows),
        w_self,
        w_neigh,
        bias.reshape(1, -1),
        upstream,
    )

    row_grads = lax.all_to_all(
        back.reshape(blocks_total, slice_width, tile_size),
        ("col", "feat"),
        split_axis=0,
        concat_axis=0,
        tiled=True,
    )

    neigh_grad, hidden_out = pl.pallas_call(
        functools.partial(backward_kernel, ncol),
        out_shape=(
            jax.ShapeDtypeStruct(neighbour_feats.shape, jnp.bfloat16),
            jax.ShapeDtypeStruct(upstream.shape, jnp.bfloat16),
        ),
        in_specs=[SMEM] * 4 + [VMEM] * 3,
        out_specs=(VMEM, ANY),
        scratch_shapes=[
            pltpu.SMEM((blocks_total,), jnp.int32),
            pltpu.VMEM((col_blocks + 1, slice_width, tile_size), jnp.float32),
            pltpu.VMEM((col_blocks + 1, slice_width, tile_size), jnp.float32),
            pltpu.SemaphoreType.DMA,
        ],
        compiler_params=params,
        name="backward",
    )(
        owner_order,
        tile_rows,
        tile_cols,
        tile_count,
        row_grads,
        pltpu.with_memory_space_constraint(tiles_kept, pltpu.VMEM),
        pltpu.with_memory_space_constraint(hidden, pltpu.VMEM),
    )
    return (hidden_out, neigh_grad)


def solution(mesh):
    in_specs = (
        P(("feat", "col"), None),
        P("feat", "col"),
        P("col", None, None),
        P("col"),
        P("col"),
        P("col"),
        P(),
        P(("feat", "col")),
        P(),
        P(),
        P(),
        P(("feat", "col"), None),
    )
    out_specs = (P(("feat", "col"), None), P("feat", "col"))
    return jax.shard_map(local, mesh=mesh, in_specs=in_specs, out_specs=out_specs, check_vma=False)
```

```python
import functools

import jax
import jax.numpy as jnp
from jax import lax
from jax.experimental import pallas as pl
from jax.experimental.pallas import tpu as pltpu
from jax.sharding import PartitionSpec as P

CHUNK = 64


def invert_order(order_ref, places, ncol, value):
    def body(feat, carry):
        for col in range(ncol):
            places[order_ref[feat * ncol + col]] = value(feat, col)
        return carry

    nfeat = order_ref.shape[0] // ncol
    lax.fori_loop(0, nfeat, body, 0, unroll=max(1, 8 // ncol))


def fetch(pairs, sems):
    copies = [
        pltpu.make_async_copy(source, target, sems.at[i])
        for i, (source, target) in enumerate(pairs)
    ]
    for copy in copies:
        copy.start()
    return copies


def block_diagonal(even, odd):
    blank = jnp.zeros_like(even)
    return jnp.concatenate(
        [jnp.concatenate([even, blank], axis=1), jnp.concatenate([blank, odd], axis=1)], axis=0
    )


def tile_copy(tiles_hbm, tiles_vmem, sems, chunk):
    window = pl.ds(chunk * CHUNK, CHUNK)
    return pltpu.make_async_copy(tiles_hbm.at[window], tiles_vmem.at[window], sems.at[chunk])


def forward_kernel(
    order_hbm,
    rows_hbm,
    cols_hbm,
    count_hbm,
    feats_hbm,
    tiles_hbm,
    partial_ref,
    kept_ref,
    order_ref,
    rows_ref,
    cols_ref,
    count_ref,
    feats_ref,
    feat_blocks,
    tiles_ref,
    places,
    small_sems,
    sems,
    *accs,
):
    slots, tile_size, _ = tiles_ref.shape
    blocks_total, slice_width, _ = partial_ref.shape
    ncol = len(accs)
    nfeat = blocks_total // ncol
    small = fetch(
        [
            (order_hbm, order_ref),
            (rows_hbm, rows_ref),
            (cols_hbm, cols_ref),
            (count_hbm, count_ref),
            (feats_hbm, feats_ref),
        ],
        small_sems,
    )
    for chunk in range(slots // CHUNK):
        tile_copy(tiles_hbm, tiles_ref, sems, chunk).start(priority=1)
    for acc in accs:
        acc[...] = jnp.zeros_like(acc)
    for copy in small:
        copy.wait()
    for block in range(feat_blocks.shape[0]):
        feat_blocks[block] = feats_ref[:, block * tile_size : (block + 1) * tile_size]
    invert_order(order_ref, places, ncol, lambda feat, col: feat)
    count = count_ref[0]

    for first in range(0, slots, 2):
        if first % CHUNK == 0:
            tile_copy(tiles_hbm, tiles_ref, sems, first // CHUNK).wait()
        pair = (first, first + 1)
        kept = [tiles_ref[slot].astype(kept_ref.dtype) for slot in pair]
        for slot, tile in zip(pair, kept):
            kept_ref[slot] = tile
        feats = [feat_blocks[cols_ref[slot]] for slot in pair]
        pieces = lax.dot_general(
            block_diagonal(*feats),
            jnp.concatenate([tile.T for tile in kept], axis=0),
            (((1,), (0,)), ((), ())),
            preferred_element_type=jnp.float32,
        )
        for i, slot in enumerate(pair):
            target = jnp.where(slot < count, places[rows_ref[slot]], nfeat)
            accs[slot % ncol][target] += pieces[i * slice_width : (i + 1) * slice_width]

    for col, acc in enumerate(accs):
        partial_ref[col * nfeat : (col + 1) * nfeat] = acc[:nfeat].astype(partial_ref.dtype)


def dense_kernel(
    got_ref,
    self_ref,
    degree_ref,
    w_self_ref,
    w_neigh_ref,
    bias_ref,
    upstream_ref,
    hidden_ref,
    back_ref,
    summed,
):
    ncol, nfeat, slice_width, tile_size = got_ref.shape
    for f in range(nfeat):
        total = got_ref[0, f].astype(jnp.float32)
        for c in range(1, ncol):
            total = total + got_ref[c, f].astype(jnp.float32)
        summed[pl.ds(f * slice_width, slice_width), :] = total
    scale = lax.rsqrt(degree_ref[...].astype(jnp.float32))
    aggregate = (summed[...] * scale).astype(jnp.bfloat16)
    pre = jnp.dot(self_ref[...], w_self_ref[...], preferred_element_type=jnp.float32)
    pre = pre + lax.dot_general(
        aggregate, w_neigh_ref[...], (((0,), (0,)), ((), ())), preferred_element_type=jnp.float32
    )
    pre = pre + bias_ref[...]
    gate = jax.nn.sigmoid(pre)
    hidden_ref[...] = (pre * gate).astype(jnp.bfloat16)
    slope = gate * (1.0 + pre * (1.0 - gate))
    dpre = (upstream_ref[...].astype(jnp.float32) * slope).astype(jnp.bfloat16)
    dagg = lax.dot_general(
        w_neigh_ref[...], dpre, (((1,), (1,)), ((), ())), preferred_element_type=jnp.float32
    )
    back = dagg * scale
    for f in range(nfeat):
        piece = back[f * slice_width : (f + 1) * slice_width].astype(jnp.bfloat16)
        for c in range(ncol):
            back_ref[c, f] = piece


def backward_kernel(
    ncol,
    order_ref,
    rows_ref,
    cols_ref,
    count_ref,
    grads_ref,
    tiles_ref,
    hidden_ref,
    out_ref,
    hidden_hbm,
    places,
    acc_even,
    acc_odd,
    hidden_sem,
):
    slots, tile_size, _ = tiles_ref.shape
    slice_width = out_ref.shape[0]
    nfeat = grads_ref.shape[0] // ncol
    leaving = pltpu.make_async_copy(hidden_ref, hidden_hbm, hidden_sem)
    leaving.start()
    invert_order(order_ref, places, ncol, lambda feat, col: col * nfeat + feat)
    accs = (acc_even, acc_odd)
    for acc in accs:
        acc[...] = jnp.zeros_like(acc)
    col_blocks = out_ref.shape[1] // tile_size
    count = count_ref[0]

    for first in range(0, slots, 2):
        even = grads_ref[places[rows_ref[first]]]
        odd = grads_ref[places[rows_ref[first + 1]]]
        pieces = lax.dot_general(
            block_diagonal(even, odd),
            tiles_ref[pl.ds(first, 2)].reshape(2 * tile_size, tile_size),
            (((1,), (0,)), ((), ())),
            preferred_element_type=jnp.float32,
        )
        for i, acc in enumerate(accs):
            target = jnp.where(first + i < count, cols_ref[first + i], col_blocks)
            acc[target] += pieces[i * slice_width : (i + 1) * slice_width]

    for block in range(col_blocks):
        total = acc_even[block] + acc_odd[block]
        out_ref[:, block * tile_size : (block + 1) * tile_size] = total.astype(out_ref.dtype)
    leaving.wait()


VMEM = pl.BlockSpec(memory_space=pltpu.VMEM)
SMEM = pl.BlockSpec(memory_space=pltpu.SMEM)
ANY = pl.BlockSpec(memory_space=pl.ANY)


def in_hbm(x):
    return pltpu.with_memory_space_constraint(x, pltpu.HBM)


def local(
    self_feats,
    neighbour_feats,
    tiles,
    tile_rows,
    tile_cols,
    tile_count,
    owner_order,
    degree,
    w_self,
    w_neigh,
    bias,
    upstream,
):
    nfeat = lax.axis_size("feat")
    ncol = lax.axis_size("col")
    slots, tile_size, _ = tiles.shape
    slice_width, width = neighbour_feats.shape
    col_blocks = width // tile_size
    rows = self_feats.shape[0]
    blocks_total = owner_order.shape[0]
    assert rows == tile_size and blocks_total == nfeat * ncol
    index_arrays = [in_hbm(x) for x in (owner_order, tile_rows, tile_cols)] + [tile_count]
    index_scratch = [pltpu.SMEM(x.shape, x.dtype) for x in index_arrays]
    params = pltpu.CompilerParams(vmem_limit_bytes=32 << 20)

    partial_value, tiles_kept = pl.pallas_call(
        forward_kernel,
        out_shape=(
            jax.ShapeDtypeStruct((blocks_total, slice_width, tile_size), jnp.bfloat16),
            pltpu.VMEM(tiles.shape, jnp.float8_e4m3fn),
        ),
        in_specs=[ANY] * 6,
        out_specs=(VMEM, VMEM),
        scratch_shapes=index_scratch
        + [
            pltpu.VMEM(neighbour_feats.shape, neighbour_feats.dtype),
            pltpu.VMEM((col_blocks, slice_width, tile_size), neighbour_feats.dtype),
            pltpu.VMEM(tiles.shape, tiles.dtype),
            pltpu.SMEM((blocks_total,), jnp.int32),
            pltpu.SemaphoreType.DMA((5,)),
            pltpu.SemaphoreType.DMA((slots // CHUNK,)),
        ]
        + [pltpu.VMEM((blocks_total // ncol + 1, slice_width, tile_size), jnp.float32)] * ncol,
        compiler_params=params,
        name="forward",
    )(*index_arrays, in_hbm(neighbour_feats), in_hbm(tiles))

    got = lax.all_to_all(partial_value, ("col", "feat"), split_axis=0, concat_axis=0, tiled=True)

    hidden, back = pl.pallas_call(
        dense_kernel,
        out_shape=(
            pltpu.VMEM(upstream.shape, jnp.bfloat16),
            jax.ShapeDtypeStruct((ncol, nfeat, slice_width, tile_size), jnp.bfloat16),
        ),
        in_specs=[VMEM] * 7,
        out_specs=(VMEM, VMEM),
        scratch_shapes=[pltpu.VMEM((nfeat * slice_width, tile_size), jnp.float32)],
        compiler_params=params,
        name="dense",
    )(
        got.reshape(ncol, nfeat, slice_width, tile_size),
        self_feats,
        degree.reshape(1, rows),
        w_self,
        w_neigh,
        bias.reshape(1, -1),
        upstream,
    )

    row_grads = lax.all_to_all(
        back.reshape(blocks_total, slice_width, tile_size),
        ("col", "feat"),
        split_axis=0,
        concat_axis=0,
        tiled=True,
    )

    neigh_grad, hidden_out = pl.pallas_call(
        functools.partial(backward_kernel, ncol),
        out_shape=(
            jax.ShapeDtypeStruct(neighbour_feats.shape, jnp.bfloat16),
            jax.ShapeDtypeStruct(upstream.shape, jnp.bfloat16),
        ),
        in_specs=[SMEM] * 4 + [VMEM] * 3,
        out_specs=(VMEM, ANY),
        scratch_shapes=[
            pltpu.SMEM((blocks_total,), jnp.int32),
            pltpu.VMEM((col_blocks + 1, slice_width, tile_size), jnp.float32),
            pltpu.VMEM((col_blocks + 1, slice_width, tile_size), jnp.float32),
            pltpu.SemaphoreType.DMA,
        ],
        compiler_params=params,
        name="backward",
    )(
        owner_order,
        tile_rows,
        tile_cols,
        tile_count,
        row_grads,
        pltpu.with_memory_space_constraint(tiles_kept, pltpu.VMEM),
        pltpu.with_memory_space_constraint(hidden, pltpu.VMEM),
    )
    return (hidden_out, neigh_grad)


def solution(mesh):
    in_specs = (
        P(("feat", "col"), None),
        P("feat", "col"),
        P("col", None, None),
        P("col"),
        P("col"),
        P("col"),
        P(),
        P(("feat", "col")),
        P(),
        P(),
        P(),
        P(("feat", "col"), None),
    )
    out_specs = (P(("feat", "col"), None), P("feat", "col"))
    return jax.shard_map(local, mesh=mesh, in_specs=in_specs, out_specs=out_specs, check_vma=False)
```

```python
import functools

import jax
import jax.numpy as jnp
from jax import lax
from jax.experimental import pallas as pl
from jax.experimental.pallas import tpu as pltpu
from jax.sharding import PartitionSpec as P

CHUNK = 32


def invert_order(order_ref, places, ncol, value):
    def body(feat, carry):
        for col in range(ncol):
            places[order_ref[feat * ncol + col]] = value(feat, col)
        return carry

    nfeat = order_ref.shape[0] // ncol
    lax.fori_loop(0, nfeat, body, 0, unroll=max(1, 8 // ncol))


def fetch(pairs, sems):
    copies = [
        pltpu.make_async_copy(source, target, sems.at[i])
        for i, (source, target) in enumerate(pairs)
    ]
    for copy in copies:
        copy.start()
    return copies


def block_diagonal(even, odd):
    blank = jnp.zeros_like(even)
    return jnp.concatenate(
        [jnp.concatenate([even, blank], axis=1), jnp.concatenate([blank, odd], axis=1)], axis=0
    )


def tile_copy(tiles_hbm, tiles_vmem, sems, chunk):
    window = pl.ds(chunk * CHUNK, CHUNK)
    return pltpu.make_async_copy(tiles_hbm.at[window], tiles_vmem.at[window], sems.at[chunk])


def forward_kernel(
    order_hbm,
    rows_hbm,
    cols_hbm,
    count_hbm,
    feats_hbm,
    tiles_hbm,
    partial_ref,
    kept_ref,
    order_ref,
    rows_ref,
    cols_ref,
    count_ref,
    feats_ref,
    feat_blocks,
    tiles_ref,
    places,
    small_sems,
    sems,
    *accs,
):
    slots, tile_size, _ = tiles_ref.shape
    blocks_total, slice_width, _ = partial_ref.shape
    ncol = len(accs)
    nfeat = blocks_total // ncol
    small = fetch(
        [
            (order_hbm, order_ref),
            (rows_hbm, rows_ref),
            (cols_hbm, cols_ref),
            (count_hbm, count_ref),
            (feats_hbm, feats_ref),
        ],
        small_sems,
    )
    for chunk in range(slots // CHUNK):
        tile_copy(tiles_hbm, tiles_ref, sems, chunk).start(priority=1)
    for acc in accs:
        acc[...] = jnp.zeros_like(acc)
    for copy in small:
        copy.wait()
    for block in range(feat_blocks.shape[0]):
        feat_blocks[block] = feats_ref[:, block * tile_size : (block + 1) * tile_size]
    invert_order(order_ref, places, ncol, lambda feat, col: feat)
    count = count_ref[0]

    for first in range(0, slots, 2):
        if first % CHUNK == 0:
            tile_copy(tiles_hbm, tiles_ref, sems, first // CHUNK).wait()
        pair = (first, first + 1)
        kept = [tiles_ref[slot].astype(kept_ref.dtype) for slot in pair]
        for slot, tile in zip(pair, kept):
            kept_ref[slot] = tile
        feats = [feat_blocks[cols_ref[slot]] for slot in pair]
        pieces = lax.dot_general(
            block_diagonal(*feats),
            jnp.concatenate([tile.T for tile in kept], axis=0),
            (((1,), (0,)), ((), ())),
            preferred_element_type=jnp.float32,
        )
        for i, slot in enumerate(pair):
            target = jnp.where(slot < count, places[rows_ref[slot]], nfeat)
            accs[slot % ncol][target] += pieces[i * slice_width : (i + 1) * slice_width]

    for col, acc in enumerate(accs):
        partial_ref[col * nfeat : (col + 1) * nfeat] = acc[:nfeat].astype(partial_ref.dtype)


def dense_kernel(
    got_ref,
    self_ref,
    degree_ref,
    w_self_ref,
    w_neigh_ref,
    bias_ref,
    upstream_ref,
    hidden_ref,
    back_ref,
    summed,
):
    ncol, nfeat, slice_width, tile_size = got_ref.shape
    for f in range(nfeat):
        total = got_ref[0, f].astype(jnp.float32)
        for c in range(1, ncol):
            total = total + got_ref[c, f].astype(jnp.float32)
        summed[pl.ds(f * slice_width, slice_width), :] = total
    scale = lax.rsqrt(degree_ref[...].astype(jnp.float32))
    aggregate = (summed[...] * scale).astype(jnp.bfloat16)
    pre = jnp.dot(self_ref[...], w_self_ref[...], preferred_element_type=jnp.float32)
    pre = pre + lax.dot_general(
        aggregate, w_neigh_ref[...], (((0,), (0,)), ((), ())), preferred_element_type=jnp.float32
    )
    pre = pre + bias_ref[...]
    gate = jax.nn.sigmoid(pre)
    hidden_ref[...] = (pre * gate).astype(jnp.bfloat16)
    slope = gate * (1.0 + pre * (1.0 - gate))
    dpre = (upstream_ref[...].astype(jnp.float32) * slope).astype(jnp.bfloat16)
    dagg = lax.dot_general(
        w_neigh_ref[...], dpre, (((1,), (1,)), ((), ())), preferred_element_type=jnp.float32
    )
    back = dagg * scale
    for f in range(nfeat):
        piece = back[f * slice_width : (f + 1) * slice_width].astype(jnp.bfloat16)
        for c in range(ncol):
            back_ref[c, f] = piece


def backward_kernel(
    ncol,
    order_ref,
    rows_ref,
    cols_ref,
    count_ref,
    grads_ref,
    tiles_ref,
    hidden_ref,
    out_ref,
    hidden_hbm,
    places,
    acc_even,
    acc_odd,
    hidden_sem,
):
    slots, tile_size, _ = tiles_ref.shape
    slice_width = out_ref.shape[0]
    nfeat = grads_ref.shape[0] // ncol
    leaving = pltpu.make_async_copy(hidden_ref, hidden_hbm, hidden_sem)
    leaving.start()
    invert_order(order_ref, places, ncol, lambda feat, col: col * nfeat + feat)
    accs = (acc_even, acc_odd)
    for acc in accs:
        acc[...] = jnp.zeros_like(acc)
    col_blocks = out_ref.shape[1] // tile_size
    count = count_ref[0]

    for first in range(0, slots, 2):
        even = grads_ref[places[rows_ref[first]]]
        odd = grads_ref[places[rows_ref[first + 1]]]
        pieces = lax.dot_general(
            block_diagonal(even, odd),
            tiles_ref[pl.ds(first, 2)].reshape(2 * tile_size, tile_size),
            (((1,), (0,)), ((), ())),
            preferred_element_type=jnp.float32,
        )
        for i, acc in enumerate(accs):
            target = jnp.where(first + i < count, cols_ref[first + i], col_blocks)
            acc[target] += pieces[i * slice_width : (i + 1) * slice_width]

    for block in range(col_blocks):
        total = acc_even[block] + acc_odd[block]
        out_ref[:, block * tile_size : (block + 1) * tile_size] = total.astype(out_ref.dtype)
    leaving.wait()


VMEM = pl.BlockSpec(memory_space=pltpu.VMEM)
SMEM = pl.BlockSpec(memory_space=pltpu.SMEM)
ANY = pl.BlockSpec(memory_space=pl.ANY)


def in_hbm(x):
    return pltpu.with_memory_space_constraint(x, pltpu.HBM)


def local(
    self_feats,
    neighbour_feats,
    tiles,
    tile_rows,
    tile_cols,
    tile_count,
    owner_order,
    degree,
    w_self,
    w_neigh,
    bias,
    upstream,
):
    nfeat = lax.axis_size("feat")
    ncol = lax.axis_size("col")
    slots, tile_size, _ = tiles.shape
    slice_width, width = neighbour_feats.shape
    col_blocks = width // tile_size
    rows = self_feats.shape[0]
    blocks_total = owner_order.shape[0]
    assert rows == tile_size and blocks_total == nfeat * ncol
    index_arrays = [in_hbm(x) for x in (owner_order, tile_rows, tile_cols)] + [tile_count]
    index_scratch = [pltpu.SMEM(x.shape, x.dtype) for x in index_arrays]
    params = pltpu.CompilerParams(vmem_limit_bytes=32 << 20)

    partial_value, tiles_kept = pl.pallas_call(
        forward_kernel,
        out_shape=(
            jax.ShapeDtypeStruct((blocks_total, slice_width, tile_size), jnp.bfloat16),
            pltpu.VMEM(tiles.shape, jnp.float8_e4m3fn),
        ),
        in_specs=[ANY] * 6,
        out_specs=(VMEM, VMEM),
        scratch_shapes=index_scratch
        + [
            pltpu.VMEM(neighbour_feats.shape, neighbour_feats.dtype),
            pltpu.VMEM((col_blocks, slice_width, tile_size), neighbour_feats.dtype),
            pltpu.VMEM(tiles.shape, tiles.dtype),
            pltpu.SMEM((blocks_total,), jnp.int32),
            pltpu.SemaphoreType.DMA((5,)),
            pltpu.SemaphoreType.DMA((slots // CHUNK,)),
        ]
        + [pltpu.VMEM((blocks_total // ncol + 1, slice_width, tile_size), jnp.float32)] * ncol,
        compiler_params=params,
        name="forward",
    )(*index_arrays, in_hbm(neighbour_feats), in_hbm(tiles))

    got = lax.all_to_all(partial_value, ("col", "feat"), split_axis=0, concat_axis=0, tiled=True)

    hidden, back = pl.pallas_call(
        dense_kernel,
        out_shape=(
            pltpu.VMEM(upstream.shape, jnp.bfloat16),
            jax.ShapeDtypeStruct((ncol, nfeat, slice_width, tile_size), jnp.bfloat16),
        ),
        in_specs=[VMEM] * 7,
        out_specs=(VMEM, VMEM),
        scratch_shapes=[pltpu.VMEM((nfeat * slice_width, tile_size), jnp.float32)],
        compiler_params=params,
        name="dense",
    )(
        got.reshape(ncol, nfeat, slice_width, tile_size),
        self_feats,
        degree.reshape(1, rows),
        w_self,
        w_neigh,
        bias.reshape(1, -1),
        upstream,
    )

    row_grads = lax.all_to_all(
        back.reshape(blocks_total, slice_width, tile_size),
        ("col", "feat"),
        split_axis=0,
        concat_axis=0,
        tiled=True,
    )

    neigh_grad, hidden_out = pl.pallas_call(
        functools.partial(backward_kernel, ncol),
        out_shape=(
            jax.ShapeDtypeStruct(neighbour_feats.shape, jnp.bfloat16),
            jax.ShapeDtypeStruct(upstream.shape, jnp.bfloat16),
        ),
        in_specs=[SMEM] * 4 + [VMEM] * 3,
        out_specs=(VMEM, ANY),
        scratch_shapes=[
            pltpu.SMEM((blocks_total,), jnp.int32),
            pltpu.VMEM((col_blocks + 1, slice_width, tile_size), jnp.float32),
            pltpu.VMEM((col_blocks + 1, slice_width, tile_size), jnp.float32),
            pltpu.SemaphoreType.DMA,
        ],
        compiler_params=params,
        name="backward",
    )(
        owner_order,
        tile_rows,
        tile_cols,
        tile_count,
        row_grads,
        pltpu.with_memory_space_constraint(tiles_kept, pltpu.VMEM),
        pltpu.with_memory_space_constraint(hidden, pltpu.VMEM),
    )
    return (hidden_out, neigh_grad)


def solution(mesh):
    in_specs = (
        P(("feat", "col"), None),
        P("feat", "col"),
        P("col", None, None),
        P("col"),
        P("col"),
        P("col"),
        P(),
        P(("feat", "col")),
        P(),
        P(),
        P(),
        P(("feat", "col"), None),
    )
    out_specs = (P(("feat", "col"), None), P("feat", "col"))
    return jax.shard_map(local, mesh=mesh, in_specs=in_specs, out_specs=out_specs, check_vma=False)
```

```python
import functools

import jax
import jax.numpy as jnp
from jax import lax
from jax.experimental import pallas as pl
from jax.experimental.pallas import tpu as pltpu
from jax.sharding import PartitionSpec as P

CHUNK = 64


def invert_order(order_ref, places, ncol, value):
    def body(feat, carry):
        for col in range(ncol):
            places[order_ref[feat * ncol + col]] = value(feat, col)
        return carry

    nfeat = order_ref.shape[0] // ncol
    lax.fori_loop(0, nfeat, body, 0, unroll=max(1, 8 // ncol))


def fetch(pairs, sems):
    copies = [
        pltpu.make_async_copy(source, target, sems.at[i])
        for i, (source, target) in enumerate(pairs)
    ]
    for copy in copies:
        copy.start()
    return copies


def block_diagonal(even, odd):
    blank = jnp.zeros_like(even)
    return jnp.concatenate(
        [jnp.concatenate([even, blank], axis=1), jnp.concatenate([blank, odd], axis=1)], axis=0
    )


def tile_copy(tiles_hbm, tiles_vmem, sems, chunk):
    window = pl.ds(chunk * CHUNK, CHUNK)
    return pltpu.make_async_copy(tiles_hbm.at[window], tiles_vmem.at[window], sems.at[chunk])


def forward_kernel(
    order_hbm,
    rows_hbm,
    cols_hbm,
    count_hbm,
    feats_hbm,
    tiles_hbm,
    partial_ref,
    kept_ref,
    order_ref,
    rows_ref,
    cols_ref,
    count_ref,
    feats_ref,
    feat_blocks,
    tiles_ref,
    places,
    small_sems,
    sems,
    *accs,
):
    slots, tile_size, _ = tiles_ref.shape
    blocks_total, slice_width, _ = partial_ref.shape
    ncol = len(accs)
    nfeat = blocks_total // ncol
    for chunk in range(slots // CHUNK):
        tile_copy(tiles_hbm, tiles_ref, sems, chunk).start(priority=1)
    small = fetch(
        [
            (order_hbm, order_ref),
            (rows_hbm, rows_ref),
            (cols_hbm, cols_ref),
            (count_hbm, count_ref),
            (feats_hbm, feats_ref),
        ],
        small_sems,
    )
    for acc in accs:
        acc[...] = jnp.zeros_like(acc)
    for copy in small:
        copy.wait()
    for block in range(feat_blocks.shape[0]):
        feat_blocks[block] = feats_ref[:, block * tile_size : (block + 1) * tile_size]
    invert_order(order_ref, places, ncol, lambda feat, col: feat)
    count = count_ref[0]

    for first in range(0, slots, 2):
        if first % CHUNK == 0:
            tile_copy(tiles_hbm, tiles_ref, sems, first // CHUNK).wait()
        pair = (first, first + 1)
        kept = [tiles_ref[slot].astype(kept_ref.dtype) for slot in pair]
        for slot, tile in zip(pair, kept):
            kept_ref[slot] = tile
        feats = [feat_blocks[cols_ref[slot]] for slot in pair]
        pieces = lax.dot_general(
            block_diagonal(*feats),
            jnp.concatenate([tile.T for tile in kept], axis=0),
            (((1,), (0,)), ((), ())),
            preferred_element_type=jnp.float32,
        )
        for i, slot in enumerate(pair):
            target = jnp.where(slot < count, places[rows_ref[slot]], nfeat)
            accs[slot % ncol][target] += pieces[i * slice_width : (i + 1) * slice_width]

    for col, acc in enumerate(accs):
        partial_ref[col * nfeat : (col + 1) * nfeat] = acc[:nfeat].astype(partial_ref.dtype)


def dense_kernel(
    got_ref,
    self_ref,
    degree_ref,
    w_self_ref,
    w_neigh_ref,
    bias_ref,
    upstream_ref,
    hidden_ref,
    back_ref,
    summed,
):
    ncol, nfeat, slice_width, tile_size = got_ref.shape
    for f in range(nfeat):
        total = got_ref[0, f].astype(jnp.float32)
        for c in range(1, ncol):
            total = total + got_ref[c, f].astype(jnp.float32)
        summed[pl.ds(f * slice_width, slice_width), :] = total
    scale = lax.rsqrt(degree_ref[...].astype(jnp.float32))
    aggregate = (summed[...] * scale).astype(jnp.bfloat16)
    pre = jnp.dot(self_ref[...], w_self_ref[...], preferred_element_type=jnp.float32)
    pre = pre + lax.dot_general(
        aggregate, w_neigh_ref[...], (((0,), (0,)), ((), ())), preferred_element_type=jnp.float32
    )
    pre = pre + bias_ref[...]
    gate = jax.nn.sigmoid(pre)
    hidden_ref[...] = (pre * gate).astype(jnp.bfloat16)
    slope = gate * (1.0 + pre * (1.0 - gate))
    dpre = (upstream_ref[...].astype(jnp.float32) * slope).astype(jnp.bfloat16)
    dagg = lax.dot_general(
        w_neigh_ref[...], dpre, (((1,), (1,)), ((), ())), preferred_element_type=jnp.float32
    )
    back = dagg * scale
    for f in range(nfeat):
        piece = back[f * slice_width : (f + 1) * slice_width].astype(jnp.bfloat16)
        for c in range(ncol):
            back_ref[c, f] = piece


def backward_kernel(
    ncol,
    order_ref,
    rows_ref,
    cols_ref,
    count_ref,
    grads_ref,
    tiles_ref,
    hidden_ref,
    out_ref,
    hidden_hbm,
    places,
    acc_even,
    acc_odd,
    hidden_sem,
):
    slots, tile_size, _ = tiles_ref.shape
    slice_width = out_ref.shape[0]
    nfeat = grads_ref.shape[0] // ncol
    leaving = pltpu.make_async_copy(hidden_ref, hidden_hbm, hidden_sem)
    leaving.start()
    invert_order(order_ref, places, ncol, lambda feat, col: col * nfeat + feat)
    accs = (acc_even, acc_odd)
    for acc in accs:
        acc[...] = jnp.zeros_like(acc)
    col_blocks = out_ref.shape[1] // tile_size
    count = count_ref[0]

    for first in range(0, slots, 2):
        even = grads_ref[places[rows_ref[first]]]
        odd = grads_ref[places[rows_ref[first + 1]]]
        pieces = lax.dot_general(
            block_diagonal(even, odd),
            tiles_ref[pl.ds(first, 2)].reshape(2 * tile_size, tile_size),
            (((1,), (0,)), ((), ())),
            preferred_element_type=jnp.float32,
        )
        for i, acc in enumerate(accs):
            target = jnp.where(first + i < count, cols_ref[first + i], col_blocks)
            acc[target] += pieces[i * slice_width : (i + 1) * slice_width]

    for block in range(col_blocks):
        total = acc_even[block] + acc_odd[block]
        out_ref[:, block * tile_size : (block + 1) * tile_size] = total.astype(out_ref.dtype)
    leaving.wait()


VMEM = pl.BlockSpec(memory_space=pltpu.VMEM)
SMEM = pl.BlockSpec(memory_space=pltpu.SMEM)
ANY = pl.BlockSpec(memory_space=pl.ANY)


def in_hbm(x):
    return pltpu.with_memory_space_constraint(x, pltpu.HBM)


def local(
    self_feats,
    neighbour_feats,
    tiles,
    tile_rows,
    tile_cols,
    tile_count,
    owner_order,
    degree,
    w_self,
    w_neigh,
    bias,
    upstream,
):
    nfeat = lax.axis_size("feat")
    ncol = lax.axis_size("col")
    slots, tile_size, _ = tiles.shape
    slice_width, width = neighbour_feats.shape
    col_blocks = width // tile_size
    rows = self_feats.shape[0]
    blocks_total = owner_order.shape[0]
    assert rows == tile_size and blocks_total == nfeat * ncol
    index_arrays = [in_hbm(x) for x in (owner_order, tile_rows, tile_cols)] + [tile_count]
    index_scratch = [pltpu.SMEM(x.shape, x.dtype) for x in index_arrays]
    params = pltpu.CompilerParams(vmem_limit_bytes=32 << 20)

    partial_value, tiles_kept = pl.pallas_call(
        forward_kernel,
        out_shape=(
            jax.ShapeDtypeStruct((blocks_total, slice_width, tile_size), jnp.bfloat16),
            pltpu.VMEM(tiles.shape, jnp.float8_e4m3fn),
        ),
        in_specs=[ANY] * 6,
        out_specs=(VMEM, VMEM),
        scratch_shapes=index_scratch
        + [
            pltpu.VMEM(neighbour_feats.shape, neighbour_feats.dtype),
            pltpu.VMEM((col_blocks, slice_width, tile_size), neighbour_feats.dtype),
            pltpu.VMEM(tiles.shape, tiles.dtype),
            pltpu.SMEM((blocks_total,), jnp.int32),
            pltpu.SemaphoreType.DMA((5,)),
            pltpu.SemaphoreType.DMA((slots // CHUNK,)),
        ]
        + [pltpu.VMEM((blocks_total // ncol + 1, slice_width, tile_size), jnp.float32)] * ncol,
        compiler_params=params,
        name="forward",
    )(*index_arrays, in_hbm(neighbour_feats), in_hbm(tiles))

    got = lax.all_to_all(partial_value, ("col", "feat"), split_axis=0, concat_axis=0, tiled=True)

    hidden, back = pl.pallas_call(
        dense_kernel,
        out_shape=(
            pltpu.VMEM(upstream.shape, jnp.bfloat16),
            jax.ShapeDtypeStruct((ncol, nfeat, slice_width, tile_size), jnp.bfloat16),
        ),
        in_specs=[VMEM] * 7,
        out_specs=(VMEM, VMEM),
        scratch_shapes=[pltpu.VMEM((nfeat * slice_width, tile_size), jnp.float32)],
        compiler_params=params,
        name="dense",
    )(
        got.reshape(ncol, nfeat, slice_width, tile_size),
        self_feats,
        degree.reshape(1, rows),
        w_self,
        w_neigh,
        bias.reshape(1, -1),
        upstream,
    )

    row_grads = lax.all_to_all(
        back.reshape(blocks_total, slice_width, tile_size),
        ("col", "feat"),
        split_axis=0,
        concat_axis=0,
        tiled=True,
    )

    neigh_grad, hidden_out = pl.pallas_call(
        functools.partial(backward_kernel, ncol),
        out_shape=(
            jax.ShapeDtypeStruct(neighbour_feats.shape, jnp.bfloat16),
            jax.ShapeDtypeStruct(upstream.shape, jnp.bfloat16),
        ),
        in_specs=[SMEM] * 4 + [VMEM] * 3,
        out_specs=(VMEM, ANY),
        scratch_shapes=[
            pltpu.SMEM((blocks_total,), jnp.int32),
            pltpu.VMEM((col_blocks + 1, slice_width, tile_size), jnp.float32),
            pltpu.VMEM((col_blocks + 1, slice_width, tile_size), jnp.float32),
            pltpu.SemaphoreType.DMA,
        ],
        compiler_params=params,
        name="backward",
    )(
        owner_order,
        tile_rows,
        tile_cols,
        tile_count,
        row_grads,
        pltpu.with_memory_space_constraint(tiles_kept, pltpu.VMEM),
        pltpu.with_memory_space_constraint(hidden, pltpu.VMEM),
    )
    return (hidden_out, neigh_grad)


def solution(mesh):
    in_specs = (
        P(("feat", "col"), None),
        P("feat", "col"),
        P("col", None, None),
        P("col"),
        P("col"),
        P("col"),
        P(),
        P(("feat", "col")),
        P(),
        P(),
        P(),
        P(("feat", "col"), None),
    )
    out_specs = (P(("feat", "col"), None), P("feat", "col"))
    return jax.shard_map(local, mesh=mesh, in_specs=in_specs, out_specs=out_specs, check_vma=False)
```
